128 devices in a mesh: rows: 8 (over x, z_lo), cols: 16 (over z_hi, y, core).
Axes of the slice: x: 4, y: 4, z: 4 (z_hi: 2, z_lo: 2; z = z_hi * 2 + z_lo), core: 2. Of those that a mesh axis runs over, the one named last changes fastest.
Arguments:
- ancestor_inv: bfloat16 [16384, 16384], P('rows', 'cols'), may hold values from -0.0625 to 0.0625
- lfactor: bfloat16 [32, 256, 6, 256], P('cols'), may hold values from -0.8984375 to 0.8984375
- struct: int32 [6, 32], replicated, may hold values from 0 to 63, as said below
- validity: int32 [6, 32], replicated, may hold values from 0 to 1, as said below
- diag_inverse: float32 [6, 256, 256], replicated, may hold values from -6 to 6
Outputs:
- column_block: bfloat16 [16384, 1536], P(('rows', 'cols'))
- diagonal_block: float32 [6, 256, 256], replicated
The draws below stay inside these ranges and needn't reach their ends.
Inputs may be any that keep to these rules, and one draw needn't show every extreme that they name: `struct`: within a supernode the 32 tile indices are distinct and increasing, and every list holds tiles 0 and 63. `validity`: every tile index of 0 to 63 is a valid entry of some supernode's list; some supernode has all 32 flags set.
All inputs are finite; a program needn't handle non-finite values.
Results may differ from the reference program's by a relative error of at most 0.001.
Values may be sent and summed in bfloat16 or wider, within the bound.
No kernel may reach another device: no remote copies, remote signals or barrier semaphores. Data moves between devices by JAX's collectives and lax.ppermute only.
A program may use at most 192 MiB of HBM per device.

```python
import jax
import jax.numpy as jnp
from jax import lax

S = 256
SUPER = 6
NT = 64
PAD = 32


def tile_lists_common(key):
    first_key, second_key, third_key = jax.random.split(jax.random.fold_in(key, 7), 3)
    noise_draw = jax.random.randint(first_key, (SUPER, NT), 0, NT)
    indices = jnp.arange(NT, dtype=jnp.int32)
    owners = jnp.arange(SUPER, dtype=jnp.int32)
    forced = (indices[None, :] % SUPER == owners[:, None]) | (indices[None, :] == 0) | (indices[None, :] == NT - 1)
    scores = (noise_draw + indices[None, :]) * NT + indices[None, :]
    scores = jnp.where(forced, 4 * NT * NT + indices[None, :], scores)
    chosen_scores, chosen = lax.top_k(scores, PAD)
    chosen = jnp.sort(chosen, axis=1).astype(jnp.int32)
    owned = chosen % SUPER == owners[:, None]
    coins = jax.random.randint(second_key, (SUPER, PAD), 0, 2)
    filled = jax.random.randint(third_key, (), 0, SUPER)
    full_row = owners[:, None] == filled
    flag_rows = (owned | (coins == 1) | full_row).astype(jnp.int32)
    return (chosen, flag_rows)


def draw_struct(key, part):
    return tile_lists_common(key)[0]


def draw_validity(key, part):
    return tile_lists_common(key)[1]


def block_levels(own_key, shape, shards, least, high):
    def one(dim, blocks):
        heights = jax.random.uniform(jax.random.fold_in(jax.random.fold_in(own_key, 6), dim), (blocks,), jnp.float32, least / len(shards), high / len(shards))
        return jnp.repeat(jnp.exp(heights), shape[dim] // blocks).reshape((-1,) + (1,) * (len(shape) - dim - 1))

    factor_of = one(*shards[0])
    for cut in shards[1:]:
        factor_of = factor_of * one(*cut)
    return factor_of


def gaussian(key, dims, scale, reach, cuts=(), kind=jnp.bfloat16):
    gain = block_levels(key, dims, cuts, -0.22, 0.18) if cuts else 1.0
    drawn = jax.random.normal(key, dims, jnp.float32) * scale * gain
    return jnp.minimum(jnp.maximum(drawn, -reach), reach).astype(kind)


def setup_inputs(seed: int = 0) -> dict:
    splits = jax.random.split(jax.random.key(seed), 6)
    return {
        "ancestor_inv": gaussian(splits[0], (NT * S, NT * S), (PAD * S) ** -0.5, 0.0625, ((0, 8), (1, 16))),
        "lfactor": gaussian(splits[1], (PAD, S, SUPER, S), 0.15, 0.8984375, ((0, 16),)),
        "struct": draw_struct(jax.random.fold_in(splits[5], 71), 0),
        "validity": draw_validity(jax.random.fold_in(splits[5], 71), 0),
        "diag_inverse": gaussian(splits[4], (SUPER, S, S), 1.0, 6.0, (), jnp.float32),
    }


def reference(ancestor_inv, lfactor, struct, validity, diag_inverse):
    indices = jnp.arange(NT, dtype=jnp.int32)
    flagged = validity > 0
    selector = ((struct[:, :, None] == indices[None, None, :]) & flagged[:, :, None]).astype(jnp.float32)
    ancestor_panel = jnp.einsum("kpt,pakb->takb", selector, lfactor.astype(jnp.float32), precision=lax.Precision.HIGHEST)
    right_side = ancestor_panel.reshape(NT * S, SUPER * S)
    updates = -jnp.dot(ancestor_inv.astype(jnp.float32), right_side, precision=lax.Precision.HIGHEST)
    row_present = jnp.max(selector, axis=1)
    masked = updates.reshape(NT, S, SUPER, S) * jnp.transpose(row_present)[:, None, :, None]
    column_block = masked.astype(jnp.bfloat16).reshape(NT * S, SUPER * S)
    diagonal_block = diag_inverse - jnp.einsum("akb,akc->kbc", ancestor_panel.reshape(NT * S, SUPER, S), updates.reshape(NT * S, SUPER, S), precision=lax.Precision.HIGHEST)
    return column_block, diagonal_block
```

```python
import functools

import jax
import jax.numpy as jnp
from jax import lax
from jax.experimental import pallas as pl
from jax.experimental.pallas import tpu as pltpu
from jax.sharding import Mesh, PartitionSpec as P

BF16 = jnp.bfloat16
F32 = jnp.float32
NX, NL, NH, NY, NC = 4, 2, 2, 4, 2
XL = ("x", "l")
HY = ("h", "y")
CORE_SWAP = [(0, 1), (1, 0)]
LEVELS = 32000.0
LOWEST = -100.0


def pick_kernel(place, where, x_ref, o_ref):
    entries, _, width = x_ref.shape
    groups, slots = o_ref.shape[:2]
    window = slots - 1
    size = width // 3
    chip, core = where[0], where[1]
    for k in range(3):
        cols = slice(k * size, (k + 1) * size)

        def tile(t):
            p = place[core * 3 + k, t]
            block = x_ref[jnp.maximum(p, 0), :, cols]
            return jnp.where(p >= 0, block, jnp.zeros_like(block))

        for s in range(window):
            block = tile(chip * window + s)
            for g in range(groups):
                o_ref[g, s, :, cols] = block
        for g in range(groups):
            o_ref[g, window, :, cols] = tile(g * window + chip)


def product_kernel(where, own_ref, other_ref, l_ref, q_ref, panel):
    groups, slots, part, width = l_ref.shape
    window = slots - 1
    half = own_ref.shape[1]
    rows = own_ref.shape[0]

    @pl.when(pl.program_id(0) == 0)
    def _():
        for s in range(window):
            for g in range(groups):
                panel[pl.ds(s * groups * part + g * part, part), :] = l_ref[g, s]

    core = where[1]
    first = pl.multiple_of(core * half, half)
    second = pl.multiple_of((1 - core) * half, half)
    acc = jnp.dot(own_ref[...], panel[pl.ds(first, half), :], preferred_element_type=F32)
    acc += jnp.dot(other_ref[...], panel[pl.ds(second, half), :], preferred_element_type=F32)
    top = jnp.max(jnp.abs(acc), axis=0, keepdims=True)
    level = jnp.maximum(jnp.ceil(jnp.log2(jnp.maximum(top, 1e-37)) + 0.01), LOWEST)
    coded = jnp.round(acc * (jnp.exp2(-level) * LEVELS))
    q_ref[0, :rows, :] = coded.astype(jnp.int32).astype(jnp.int16)
    q_ref[0, rows:, :] = jnp.broadcast_to(level, (16, width)).astype(jnp.int32).astype(jnp.int16)


def finish_kernel(place, where, q_ref, l_ref, u_ref, d_ref):
    parts, _, width = q_ref.shape
    groups, slots, part, _ = l_ref.shape
    window = slots - 1
    rows = groups * part
    size = width // 3
    chip, core, group = where[0], where[1], where[2]
    mine = group * window + chip
    for k in range(3):
        cols = slice(k * size, (k + 1) * size)
        total = jnp.zeros((rows, size), F32)
        for j in range(parts):
            level = q_ref[j, rows : rows + 16, cols].astype(jnp.int32).astype(F32)[:1]
            total += q_ref[j, :rows, cols].astype(jnp.int32).astype(F32) * (
                jnp.exp2(level) * (1.0 / LEVELS)
            )
        update = -total
        keep = place[core * 3 + k, mine] >= 0
        u_ref[:, cols] = jnp.where(keep, update, jnp.zeros_like(update)).astype(BF16)
        own = jnp.concatenate([l_ref[g, slots - 1, :, cols] for g in range(groups)], axis=0)
        rest = update
        block = jnp.zeros((size, size), F32)
        for _ in range(3):
            high = rest.astype(BF16)
            rest = rest - high.astype(F32)
            block += lax.dot_general(
                own, high, (((0,), (0,)), ((), ())), preferred_element_type=F32
            )
        for i in range(2):
            d_ref[:, k * size + i * 128 : k * size + (i + 1) * 128] = block[:, i * 128 : (i + 1) * 128]


def body(ancestor_inv, lfactor, struct, validity, diag_inverse):
    rows, cols = ancestor_inv.shape
    entries, size, supers, _ = lfactor.shape
    groups = NX * NL
    chips = NH * NY
    part = size // groups
    width = supers // 2 * size
    group = lax.axis_index(XL)
    chip = lax.axis_index(HY)
    core = lax.axis_index("c")
    tiles = struct.shape[1] * 2
    window = tiles // chips
    smem = pl.BlockSpec(memory_space=pltpu.SMEM)
    vmem = pl.BlockSpec(memory_space=pltpu.VMEM)

    other = lax.ppermute(ancestor_inv, "c", CORE_SWAP)

    hits = (struct[:, :, None] == jnp.arange(tiles, dtype=jnp.int32)) & (validity[:, :, None] > 0)
    position = jnp.arange(struct.shape[1], dtype=jnp.int32)[None, :, None]
    place = jnp.max(jnp.where(hits, position, -1), axis=1)
    where = jnp.stack([chip, core, group]).astype(jnp.int32)

    share = lax.dynamic_slice_in_dim(lfactor, group * part, part, 1)
    share = share.reshape(entries, part, 2, width)
    share = jnp.transpose(share, (2, 0, 1, 3))
    share = jnp.broadcast_to(share[None], (chips, 2, entries, part, width))
    share = share.reshape(chips * 2, entries, part, width)
    share = lax.all_to_all(share, ("h", "y", "c"), split_axis=0, concat_axis=0, tiled=True)
    share = share.reshape(chips * 2 * entries, part, width)

    picked = pl.pallas_call(
        pick_kernel,
        out_shape=jax.ShapeDtypeStruct((groups, window + 1, part, width), BF16),
        in_specs=[smem, smem, vmem],
        out_specs=vmem,
        name="pick",
    )(place, where, share)
    picked = lax.all_to_all(picked, XL, split_axis=0, concat_axis=0, tiled=True)

    block = rows // chips
    coded = pl.pallas_call(
        product_kernel,
        grid=(chips,),
        out_shape=jax.ShapeDtypeStruct((chips, block + 16, width), jnp.int16),
        in_specs=[
            smem,
            pl.BlockSpec((block, cols), lambda i: (i, 0)),
            pl.BlockSpec((block, cols), lambda i: (i, 0)),
            vmem,
        ],
        out_specs=pl.BlockSpec((1, block + 16, width), lambda i: (i, 0, 0)),
        scratch_shapes=[pltpu.VMEM((2 * cols, width), BF16)],
        name="product",
    )(where, ancestor_inv, other, picked)
    coded = lax.all_to_all(coded, HY, split_axis=0, concat_axis=0, tiled=True)

    updates, diag = pl.pallas_call(
        finish_kernel,
        out_shape=[
            jax.ShapeDtypeStruct((block, width), BF16),
            jax.ShapeDtypeStruct((size, width), F32),
        ],
        in_specs=[smem, smem, vmem, vmem],
        out_specs=[vmem, vmem],
        name="finish",
    )(place, where, coded, picked)

    slab = block // 2
    mine = lax.dynamic_slice_in_dim(updates, core * slab, slab, 0)
    theirs = lax.dynamic_slice_in_dim(updates, (1 - core) * slab, slab, 0)
    theirs = lax.ppermute(theirs, "c", CORE_SWAP)
    column_block = jnp.where(
        core == 0,
        jnp.concatenate([mine, theirs], axis=1),
        jnp.concatenate([theirs, mine], axis=1),
    )

    pieces = groups * chips
    diag = diag.reshape(pieces, size // pieces, width)
    diag = lax.all_to_all(diag, ("x", "l", "h", "y"), split_axis=0, concat_axis=0, tiled=True)
    piece = jnp.sum(diag, axis=0)
    piece = jnp.broadcast_to(piece[None], (pieces * 2,) + piece.shape)
    whole = lax.all_to_all(piece, ("x", "l", "h", "y", "c"), split_axis=0, concat_axis=0, tiled=True)
    whole = whole.reshape(pieces, 2, size // pieces, supers // 2, size)
    whole = jnp.transpose(whole, (1, 3, 0, 2, 4)).reshape(supers, size, size)
    return column_block, diag_inverse - whole


def solution(mesh):
    fine = Mesh(mesh.devices.reshape(NX, NL, NH, NY, NC), ("x", "l", "h", "y", "c"))
    return jax.shard_map(
        body,
        mesh=fine,
        in_specs=(P(XL, ("h", "y", "c")), P(("h", "y", "c")), P(), P(), P()),
        out_specs=(P(("x", "l", "h", "y", "c")), P()),
        check_vma=False,
    )
```

```python
import jax
import jax.numpy as jnp
from jax import lax
from jax.experimental import pallas as pl
from jax.experimental.pallas import tpu as pltpu
from jax.sharding import Mesh, PartitionSpec as P

BF16 = jnp.bfloat16
F32 = jnp.float32
I16 = jnp.int16
NX, NL, NH, NY, NC = 4, 2, 2, 4, 2
XL = ("x", "l")
HY = ("h", "y")
CORE_SWAP = [(0, 1), (1, 0)]
UP = [(i, (i + 1) % NX) for i in range(NX)]
DOWN = [(i, (i - 1) % NX) for i in range(NX)]
LEVELS = 32000.0
LOWEST = -100.0
LANES = 128


def level_of(top):
    return jnp.maximum(jnp.ceil(jnp.log2(jnp.maximum(top, 1e-37)) + 0.01), LOWEST)


def code(values, level):
    return jnp.round(values * (jnp.exp2(-level) * LEVELS)).astype(jnp.int32).astype(I16)


def plain(coded):
    return coded.astype(jnp.int32).astype(F32)


def scale_of(level):
    return jnp.exp2(level) * (1.0 / LEVELS)


def pick_kernel(place, where, x_ref, low_ref, high_ref, own_ref):
    half = low_ref.shape[0]
    groups = own_ref.shape[0]
    members = x_ref.shape[1]
    chip, core = where[0], where[1]
    for k in range(members):

        def tile(t):
            return x_ref[jnp.maximum(place[core * members + k, t], 0), k]

        for s in range(half):
            low_ref[s, k] = tile(chip * 2 * half + s)
            high_ref[s, k] = tile(chip * 2 * half + half + s)
        for g in range(groups):
            own_ref[g, k] = tile(g * 2 * half + chip)


def product_kernel(place, where, own_ref, other_ref, *refs):
    parts, (q_ref, panel, acc) = refs[:-3], refs[-3:]
    half, members, part, size = parts[0].shape
    window = 2 * half
    chip, core, group, x, l = (where[i] for i in range(5))
    step = pl.program_id(0)

    @pl.when(step == 0)
    def _():
        for side in range(NL):
            for hop, shift in enumerate((0, NX - 1, 1, 2)):
                source = lax.rem(x + shift, NX) * NL + lax.rem(l + side, NL)
                for h in range(2):
                    ref = parts[(side * 4 + hop) * 2 + h]
                    for s in range(half):
                        start = pl.multiple_of((h * half + s) * size + source * part, part)
                        for k in range(members):
                            panel[k, pl.ds(start, part), :] = ref[s, k]

    for k in range(members):
        cols = slice(k * size, (k + 1) * size)
        node = core * members + k
        wanted = place[node, group * window + step] >= 0

        @pl.when(wanted)
        def _():
            acc[...] = jnp.zeros_like(acc)
            for ref, base in ((own_ref, core * half), (other_ref, (1 - core) * half)):
                for j in range(half):
                    s = base + j

                    @pl.when(place[node, chip * window + s] >= 0)
                    def _():
                        start = pl.multiple_of(s * size, size)
                        acc[...] += jnp.dot(
                            ref[:, j * size : (j + 1) * size],
                            panel[k, pl.ds(start, size), :],
                            preferred_element_type=F32,
                        )

            values = acc[...]
            level = level_of(jnp.max(jnp.abs(values), axis=0, keepdims=True))
            q_ref[0, :size, cols] = code(values, level)
            q_ref[0, size:, cols] = jnp.broadcast_to(level, (16, size)).astype(jnp.int32).astype(I16)

        @pl.when(jnp.logical_not(wanted))
        def _():
            q_ref[0, :, cols] = jnp.zeros((size + 16, size), I16)


def finish_kernel(place, where, q_ref, l_ref, u_ref, swap_ref, d_ref, block):
    sources = q_ref.shape[0]
    groups, members, part, size = l_ref.shape
    slab = u_ref.shape[0]
    chip, core, group = where[0], where[1], where[2]
    mine = group * sources + chip
    for k in range(members):
        cols = slice(k * size, (k + 1) * size)
        total = jnp.zeros((size, size), F32)
        for j in range(sources):
            scale = scale_of(plain(q_ref[j, size : size + 16, cols])[:1])
            total += plain(q_ref[j, :size, cols]) * scale
        keep = place[core * members + k, mine] >= 0
        update = jnp.where(keep, -total, jnp.zeros_like(total))
        rounded = update.astype(BF16)
        first = core == 0
        u_ref[:, cols] = jnp.where(first, rounded[:slab], rounded[slab:])
        swap_ref[:, cols] = jnp.where(first, rounded[slab:], rounded[:slab])
        own = jnp.concatenate([l_ref[g, k] for g in range(groups)], axis=0)
        rest = update
        sum_k = jnp.zeros((size, size), F32)
        for _ in range(3):
            high = rest.astype(BF16)
            rest = rest - high.astype(F32)
            sum_k += lax.dot_general(own, high, (((0,), (0,)), ((), ())), preferred_element_type=F32)
        block[:, cols] = sum_k
    values = block[...]
    level = level_of(jnp.max(jnp.abs(values), keepdims=True))
    width = values.shape[1] // 2
    for i in range(2):
        d_ref[i, :, :width] = code(values[:, i * width : (i + 1) * width], level)
        d_ref[i, :, width:] = jnp.broadcast_to(level, (size, LANES)).astype(jnp.int32).astype(I16)


def piece_kernel(q_ref, o_ref):
    width = q_ref.shape[2] - LANES
    scale = scale_of(plain(q_ref[:, :, width:]))
    sums = [
        jnp.sum(plain(q_ref[:, :, i : i + LANES]) * scale, axis=0) for i in range(0, width, LANES)
    ]
    values = jnp.concatenate(sums, axis=1)
    level = level_of(jnp.max(jnp.abs(values), keepdims=True))
    coded = jnp.concatenate(
        [
            code(values, level),
            jnp.broadcast_to(level, (values.shape[0], LANES)).astype(jnp.int32).astype(I16),
        ],
        axis=1,
    )
    for j in range(o_ref.shape[0]):
        o_ref[j] = coded


def diagonal_kernel(q_ref, inverse_ref, o_ref):
    pieces, cores, depth, _ = q_ref.shape
    supers, size, _ = inverse_ref.shape
    width = q_ref.shape[3] - LANES
    count = pieces // 2
    for c in range(cores):
        for i in range(2):
            rows = slice(i * count, (i + 1) * count)
            scale = scale_of(plain(q_ref[rows, c, :, width:]))
            for t in range(width // LANES):
                lane = (i * width + t * LANES) % size
                k = c * (supers // cores) + (i * width + t * LANES) // size
                values = plain(q_ref[rows, c, :, t * LANES : (t + 1) * LANES]) * scale
                values = values.reshape(count * depth, LANES)
                o_ref[k, :, lane : lane + LANES] = (
                    inverse_ref[k, :, lane : lane + LANES] - values
                )


def spread(own):
    low, high = own
    below = [lax.ppermute(v, "x", UP) for v in (low, high)]
    above = [lax.ppermute(v, "x", DOWN) for v in (low, high)]
    far = [lax.ppermute(below[0], "x", UP), lax.ppermute(above[1], "x", DOWN)]
    return [low, high, *below, *above, *far]


def body(ancestor_inv, lfactor, struct, validity, diag_inverse):
    rows, cols = ancestor_inv.shape
    entries, size, supers, _ = lfactor.shape
    groups = NX * NL
    chips = NH * NY
    part = size // groups
    members = supers // NC
    width = members * size
    group = lax.axis_index(XL)
    chip = lax.axis_index(HY)
    core = lax.axis_index("c")
    listed = struct.shape[1]
    tiles = rows * groups // size
    window = tiles // chips
    smem = pl.BlockSpec(memory_space=pltpu.SMEM)
    vmem = pl.BlockSpec(memory_space=pltpu.VMEM)

    other = lax.ppermute(ancestor_inv, "c", CORE_SWAP)

    hits = (struct[:, :, None] == jnp.arange(tiles, dtype=jnp.int32)) & (validity[:, :, None] > 0)
    position = jnp.arange(listed, dtype=jnp.int32)[None, :, None]
    place = jnp.max(jnp.where(hits, position, -1), axis=1)
    where = jnp.stack([chip, core, group, lax.axis_index("x"), lax.axis_index("l")])

    share = jnp.transpose(lfactor, (0, 2, 1, 3))
    share = lax.dynamic_slice_in_dim(share, group * part, part, 2)
    share = share.reshape(entries, NC, members, part, size)
    share = jnp.transpose(share, (1, 0, 2, 3, 4))
    share = jnp.broadcast_to(share[None], (chips,) + share.shape)
    share = share.reshape((chips * NC,) + share.shape[2:])
    share = lax.all_to_all(share, ("h", "y", "c"), split_axis=0, concat_axis=0, tiled=True)
    share = share.reshape(listed, members, part, size)

    half = jax.ShapeDtypeStruct((window // 2, members, part, size), BF16)
    low, high, own = pl.pallas_call(
        pick_kernel,
        out_shape=[half, half, jax.ShapeDtypeStruct((groups, members, part, size), BF16)],
        in_specs=[smem, smem, vmem],
        out_specs=[vmem] * 3,
        name="pick",
    )(place, where, share)
    across = [lax.ppermute(v, "l", CORE_SWAP) for v in (low, high)]
    window_parts = spread((low, high)) + spread(across)
    own = lax.all_to_all(own, XL, split_axis=0, concat_axis=0, tiled=True)

    coded = pl.pallas_call(
        product_kernel,
        grid=(chips,),
        out_shape=jax.ShapeDtypeStruct((chips, size + 16, width), I16),
        in_specs=[smem, smem]
        + [pl.BlockSpec((size, cols), lambda i: (i, 0))] * 2
        + [vmem] * len(window_parts),
        out_specs=pl.BlockSpec((1, size + 16, width), lambda i: (i, 0, 0)),
        scratch_shapes=[
            pltpu.VMEM((members, window * size, size), BF16),
            pltpu.VMEM((size, size), F32),
        ],
        name="product",
    )(place, where, ancestor_inv, other, *window_parts)
    coded = lax.all_to_all(coded, HY, split_axis=0, concat_axis=0, tiled=True)

    slab = jax.ShapeDtypeStruct((size // NC, width), BF16)
    pieces = groups * chips
    depth = 2 * size // pieces
    reach = width // 2 + LANES
    mine, theirs, diag = pl.pallas_call(
        finish_kernel,
        out_shape=[slab, slab, jax.ShapeDtypeStruct((2, size, reach), I16)],
        in_specs=[smem, smem, vmem, vmem],
        out_specs=[vmem] * 3,
        scratch_shapes=[pltpu.VMEM((size, width), F32)],
        name="finish",
    )(place, where, coded, own)

    theirs = lax.ppermute(theirs, "c", CORE_SWAP)
    column_block = jnp.where(
        core == 0,
        jnp.concatenate([mine, theirs], axis=1),
        jnp.concatenate([theirs, mine], axis=1),
    )

    diag = diag.reshape(pieces, depth, reach)
    diag = lax.all_to_all(diag, ("x", "l", "h", "y"), split_axis=0, concat_axis=0, tiled=True)
    piece = pl.pallas_call(
        piece_kernel,
        out_shape=jax.ShapeDtypeStruct((pieces * NC, depth, reach), I16),
        in_specs=[vmem],
        out_specs=vmem,
        name="piece",
    )(diag)
    whole = lax.all_to_all(piece, ("x", "l", "h", "y", "c"), split_axis=0, concat_axis=0, tiled=True)
    diagonal = pl.pallas_call(
        diagonal_kernel,
        out_shape=jax.ShapeDtypeStruct(diag_inverse.shape, F32),
        in_specs=[vmem, vmem],
        out_specs=vmem,
        name="diagonal",
    )(whole.reshape(pieces, NC, depth, reach), diag_inverse)
    return column_block, diagonal


def solution(mesh):
    fine = Mesh(mesh.devices.reshape(NX, NL, NH, NY, NC), ("x", "l", "h", "y", "c"))
    return jax.shard_map(
        body,
        mesh=fine,
        in_specs=(P(XL, ("h", "y", "c")), P(("h", "y", "c")), P(), P(), P()),
        out_specs=(P(("x", "l", "h", "y", "c")), P()),
        check_vma=False,
    )
```

```python
import jax
import jax.numpy as jnp
from jax import lax
from jax.experimental import pallas as pl
from jax.experimental.pallas import tpu as pltpu
from jax.sharding import Mesh, PartitionSpec as P


BF16 = jnp.bfloat16
F32 = jnp.float32
I16 = jnp.int16
NX, NL, NH, NY, NC = 4, 2, 2, 4, 2
XL = ("x", "l")
HY = ("h", "y")
CHIPS = XL + HY
CORE_SWAP = [(0, 1), (1, 0)]
UP = [(i, (i + 1) % NX) for i in range(NX)]
DOWN = [(i, (i - 1) % NX) for i in range(NX)]
LEVELS = 32000.0
LOWEST = -100.0
LANES = 128


def level_of(top):
    return jnp.maximum(jnp.ceil(jnp.log2(jnp.maximum(top, 1e-37)) + 0.01), LOWEST)


def code(values, level):
    return jnp.round(values * (jnp.exp2(-level) * LEVELS)).astype(jnp.int32).astype(I16)


def plain(coded):
    return coded.astype(jnp.int32).astype(F32)


def scale_of(level):
    return jnp.exp2(level) * (1.0 / LEVELS)


def pick_kernel(place, where, x_ref, window_ref, own_ref):
    window = window_ref.shape[0]
    groups = own_ref.shape[0]
    members = x_ref.shape[1]
    chip, core = where[0], where[1]
    for k in range(members):

        def tile(t):
            return x_ref[jnp.maximum(place[core * members + k, t], 0), k]

        for s in range(window):
            window_ref[s, k] = tile(chip * window + s)
        for g in range(groups):
            own_ref[g, k] = tile(g * window + chip)


def product_kernel(place, where, own_ref, other_ref, *refs):
    parts, (q_ref, panel, acc) = refs[:-3], refs[-3:]
    window, members, part, size = parts[0].shape
    half = window // 2
    chip, core, group, x, l = (where[i] for i in range(5))
    step = pl.program_id(0)
    h, y = where[5], where[6]
    tile = group * window + lax.rem(h + step // NY, NH) * NY + lax.rem(y + step, NY)

    @pl.when(step == 0)
    def _():
        for side in range(NL):
            for shift, h, ref, base in halves_of(parts[side * 5 : side * 5 + 5]):
                source = lax.rem(x + shift, NX) * NL + lax.rem(l + side, NL)
                for s in range(half):
                    start = pl.multiple_of((h * half + s) * size + source * part, part)
                    for k in range(members):
                        panel[k, pl.ds(start, part), :] = ref[base + s, k]

    for k in range(members):
        cols = slice(k * size, (k + 1) * size)
        node = core * members + k
        wanted = place[node, tile] >= 0

        @pl.when(wanted)
        def _():
            acc[...] = jnp.zeros_like(acc)
            for ref, base in ((own_ref, core * half), (other_ref, (1 - core) * half)):
                for j in range(half):
                    s = base + j

                    @pl.when(place[node, chip * window + s] >= 0)
                    def _():
                        start = pl.multiple_of(s * size, size)
                        acc[...] += jnp.dot(
                            ref[:, j * size : (j + 1) * size],
                            panel[k, pl.ds(start, size), :],
                            preferred_element_type=F32,
                        )

            values = acc[...]
            level = level_of(jnp.max(jnp.abs(values), axis=0, keepdims=True))
            q_ref[0, :size, cols] = code(values, level)
            q_ref[0, size:, cols] = jnp.broadcast_to(level, (16, size)).astype(jnp.int32).astype(I16)

        @pl.when(jnp.logical_not(wanted))
        def _():
            q_ref[0, :, cols] = jnp.zeros((size + 16, size), I16)


def diagonal_kernel(place, where, q_ref, *refs):
    parts, (d_ref, block) = refs[:-2], refs[-2:]
    count, members, part, size = parts[0].shape
    sources = q_ref.shape[0]
    depth = count // 2 * part
    core, group, h, y = where[1], where[2], where[5], where[6]
    block[...] = jnp.zeros_like(block)
    for side in range(NH):
        for shift, i, ref, base in halves_of(parts[side * 5 : side * 5 + 5]):
            tile = lax.rem(h + side, NH) * NY + lax.rem(y + shift, NY)
            j = side * NY + shift
            for k in range(members):
                cols = slice(k * size, (k + 1) * size)

                @pl.when(place[core * members + k, group * sources + tile] >= 0)
                def _():
                    total = jnp.zeros((size, size), F32)
                    own = ref[base : base + count // 2, k].reshape(depth, size)
                    rest = plain(q_ref[j, i * depth : (i + 1) * depth, cols])
                    for _ in range(2):
                        high = rest.astype(BF16)
                        rest = rest - high.astype(F32)
                        total += lax.dot_general(
                            own, high, (((0,), (0,)), ((), ())), preferred_element_type=F32
                        )
                    scale = scale_of(plain(q_ref[j, size : size + 16, cols])[:1])
                    block[:, cols] -= total * scale

    values = block[...]
    level = level_of(jnp.max(jnp.abs(values), keepdims=True))
    width = values.shape[1] // 2
    for i in range(2):
        d_ref[i, :, :width] = code(values[:, i * width : (i + 1) * width], level)
        d_ref[i, :, width:] = jnp.broadcast_to(level, (size, LANES)).astype(jnp.int32).astype(I16)


def finish_kernel(place, where, *refs):
    parts, (u_ref, swap_ref) = refs[:-2], refs[-2:]
    sources = len(parts)
    slab, width = u_ref.shape
    size = 2 * slab
    members = width // size
    chip, core, group = where[0], where[1], where[2]
    mine = group * sources + chip
    for k in range(members):
        cols = slice(k * size, (k + 1) * size)
        total = jnp.zeros((size, size), F32)
        for ref in parts:
            scale = scale_of(plain(ref[size : size + 16, cols])[:1])
            total += plain(ref[:size, cols]) * scale
        keep = place[core * members + k, mine] >= 0
        rounded = jnp.where(keep, -total, jnp.zeros_like(total)).astype(BF16)
        first = core == 0
        u_ref[:, cols] = jnp.where(first, rounded[:slab], rounded[slab:])
        swap_ref[:, cols] = jnp.where(first, rounded[slab:], rounded[:slab])


def piece_kernel(q_ref, o_ref):
    width = q_ref.shape[2] - LANES
    scale = scale_of(plain(q_ref[:, :, width:]))
    sums = [
        jnp.sum(plain(q_ref[:, :, i : i + LANES]) * scale, axis=0) for i in range(0, width, LANES)
    ]
    values = jnp.concatenate(sums, axis=1)
    level = level_of(jnp.max(jnp.abs(values), keepdims=True))
    coded = jnp.concatenate(
        [
            code(values, level),
            jnp.broadcast_to(level, (values.shape[0], LANES)).astype(jnp.int32).astype(I16),
        ],
        axis=1,
    )
    for j in range(o_ref.shape[0]):
        o_ref[j] = coded


def total_kernel(q_ref, inverse_ref, o_ref):
    pieces, cores, depth, _ = q_ref.shape
    supers, size, _ = inverse_ref.shape
    width = q_ref.shape[3] - LANES
    count = pieces // 2
    for c in range(cores):
        for i in range(2):
            rows = slice(i * count, (i + 1) * count)
            scale = scale_of(plain(q_ref[rows, c, :, width:]))
            for t in range(width // LANES):
                lane = (i * width + t * LANES) % size
                k = c * (supers // cores) + (i * width + t * LANES) // size
                values = plain(q_ref[rows, c, :, t * LANES : (t + 1) * LANES]) * scale
                values = values.reshape(count * depth, LANES)
                o_ref[k, :, lane : lane + LANES] = (
                    inverse_ref[k, :, lane : lane + LANES] - values
                )


def spread(own, axis):
    half = own.shape[0] // 2
    below = lax.ppermute(own, axis, UP)
    above = lax.ppermute(own, axis, DOWN)
    low = lax.ppermute(below[:half], axis, UP)
    high = lax.ppermute(above[half:], axis, DOWN)
    return [own, below, above, low, high]


def halves_of(parts):
    own, below, above, low, high = parts
    for shift, ref in ((0, own), (NX - 1, below), (1, above)):
        for h in range(2):
            yield shift, h, ref, h * (ref.shape[0] // 2)
    yield 2, 0, low, 0
    yield 2, 1, high, 0


def update(ancestor_inv, lfactor, struct, validity, diag_inverse):
    rows, cols = ancestor_inv.shape
    entries, size, supers, _ = lfactor.shape
    groups = NX * NL
    chips = NH * NY
    part = size // groups
    members = supers // NC
    width = members * size
    group = lax.axis_index(XL)
    chip = lax.axis_index(HY)
    core = lax.axis_index("c")
    listed = struct.shape[1]
    tiles = rows * groups // size
    window = tiles // chips
    smem = pl.BlockSpec(memory_space=pltpu.SMEM)
    vmem = pl.BlockSpec(memory_space=pltpu.VMEM)

    other = lax.ppermute(ancestor_inv, "c", CORE_SWAP)

    hits = (struct[:, :, None] == jnp.arange(tiles, dtype=jnp.int32)) & (validity[:, :, None] > 0)
    position = jnp.arange(listed, dtype=jnp.int32)[None, :, None]
    place = jnp.max(jnp.where(hits, position, -1), axis=1)
    where = jnp.stack([chip, core, group] + [lax.axis_index(a) for a in ("x", "l", "h", "y")])

    share = jnp.transpose(lfactor, (0, 2, 1, 3))
    share = lax.dynamic_slice_in_dim(share, group * part, part, 2)
    share = share.reshape(entries, NC, members, part, size)
    share = jnp.transpose(share, (1, 0, 2, 3, 4))
    share = jnp.broadcast_to(share[None], (chips,) + share.shape)
    share = share.reshape((chips * NC,) + share.shape[2:])
    share = lax.all_to_all(share, ("h", "y", "c"), split_axis=0, concat_axis=0, tiled=True)
    share = share.reshape(listed, members, part, size)

    block = jax.ShapeDtypeStruct((window, members, part, size), BF16)
    near, own = pl.pallas_call(
        pick_kernel,
        out_shape=[block, jax.ShapeDtypeStruct((groups, members, part, size), BF16)],
        in_specs=[smem, smem, vmem],
        out_specs=[vmem] * 2,
        name="pick",
    )(place, where, share)
    across = lax.ppermute(near, "l", CORE_SWAP)
    window_parts = spread(near, "x")
    window_parts += spread(across, "x")
    own = lax.all_to_all(own, XL, split_axis=0, concat_axis=0, tiled=True)
    across = lax.ppermute(own, "h", CORE_SWAP)
    row_parts = spread(own, "y")
    row_parts += spread(across, "y")

    def row_tile(j, _, where):
        return lax.rem(where[5] + j // NY, NH) * NY + lax.rem(where[6] + j, NY), 0

    coded = pl.pallas_call(
        product_kernel,
        out_shape=jax.ShapeDtypeStruct((chips, size + 16, width), I16),
        grid_spec=pltpu.PrefetchScalarGridSpec(
            num_scalar_prefetch=2,
            grid=(chips,),
            in_specs=[pl.BlockSpec((size, cols), row_tile)] * 2 + [vmem] * len(window_parts),
            out_specs=pl.BlockSpec((1, size + 16, width), lambda i, *_: (i, 0, 0)),
            scratch_shapes=[
                pltpu.VMEM((members, window * size, size), BF16),
                pltpu.VMEM((size, size), F32),
            ],
        ),
        name="product",
    )(place, where, ancestor_inv, other, *window_parts)
    pieces = groups * chips
    depth = 2 * size // pieces
    reach = width // 2 + LANES
    diag = pl.pallas_call(
        diagonal_kernel,
        out_shape=jax.ShapeDtypeStruct((2, size, reach), I16),
        in_specs=[smem, smem] + [vmem] * (1 + len(row_parts)),
        out_specs=vmem,
        scratch_shapes=[pltpu.VMEM((size, width), F32)],
        name="diagonal",
    )(place, where, coded, *row_parts)

    sums = [coded[0]]
    for j in (6, 5, 7, 2, 4, 1, 3):
        to = [
            (h * NY + y, (h + j // NY) % NH * NY + (y + j) % NY)
            for h in range(NH)
            for y in range(NY)
        ]
        sums.append(lax.ppermute(coded[j], HY, to))
    slab = jax.ShapeDtypeStruct((size // NC, width), BF16)
    mine, theirs = pl.pallas_call(
        finish_kernel,
        out_shape=[slab, slab],
        in_specs=[smem, smem] + [vmem] * len(sums),
        out_specs=[vmem] * 2,
        name="finish",
    )(place, where, *sums)

    theirs = lax.ppermute(theirs, "c", CORE_SWAP)
    column_block = jnp.where(
        core == 0,
        jnp.concatenate([mine, theirs], axis=1),
        jnp.concatenate([theirs, mine], axis=1),
    )

    diag = diag.reshape(pieces, depth, reach)
    diag = lax.all_to_all(diag, CHIPS, split_axis=0, concat_axis=0, tiled=True)
    piece = pl.pallas_call(
        piece_kernel,
        out_shape=jax.ShapeDtypeStruct((pieces * NC, depth, reach), I16),
        in_specs=[vmem],
        out_specs=vmem,
        name="piece",
    )(diag)
    whole = lax.all_to_all(piece, CHIPS + ("c",), split_axis=0, concat_axis=0, tiled=True)
    diagonal = pl.pallas_call(
        total_kernel,
        out_shape=jax.ShapeDtypeStruct(diag_inverse.shape, F32),
        in_specs=[vmem, vmem],
        out_specs=vmem,
        name="total",
    )(whole.reshape(pieces, NC, depth, reach), diag_inverse)
    return column_block, diagonal


def solution(mesh):
    fine = Mesh(mesh.devices.reshape(NX, NL, NH, NY, NC), ("x", "l", "h", "y", "c"))
    return jax.shard_map(
        update,
        mesh=fine,
        in_specs=(P(XL, ("h", "y", "c")), P(("h", "y", "c")), P(), P(), P()),
        out_specs=(P(("x", "l", "h", "y", "c")), P()),
        check_vma=False,
    )
```

```python
import jax
import jax.numpy as jnp
from jax import lax
from jax.experimental import pallas as pl
from jax.experimental.pallas import tpu as pltpu
from jax.sharding import Mesh, PartitionSpec as P


BF16 = jnp.bfloat16
F32 = jnp.float32
I16 = jnp.int16
NX, NL, NH, NY, NC = 4, 2, 2, 4, 2
XL = ("x", "l")
HY = ("h", "y")
CHIPS = XL + HY
CORE_SWAP = [(0, 1), (1, 0)]
UP = [(i, (i + 1) % NX) for i in range(NX)]
DOWN = [(i, (i - 1) % NX) for i in range(NX)]
LEVELS = 32000.0
LOWEST = -100.0
LANES = 128


def level_of(top):
    return jnp.maximum(jnp.ceil(jnp.log2(jnp.maximum(top, 1e-37)) + 0.01), LOWEST)


def code(values, level):
    return jnp.round(values * (jnp.exp2(-level) * LEVELS)).astype(jnp.int32).astype(I16)


def plain(coded):
    return coded.astype(jnp.int32).astype(F32)


def scale_of(level):
    return jnp.exp2(level) * (1.0 / LEVELS)


def pick_kernel(place, where, x_ref, window_ref, own_ref):
    members, window = window_ref.shape[:2]
    groups = own_ref.shape[0]
    chip, core = where[0], where[1]
    for k in range(members):

        def tile(t):
            p = place[core * members + k, t]
            block = x_ref[jnp.maximum(p, 0), k]
            return jnp.where(p >= 0, block, jnp.zeros_like(block))

        for s in range(window):
            window_ref[k, s] = tile(chip * window + s)
        for g in range(groups):
            own_ref[g, k] = tile(g * window + chip)


def product_kernel(place, where, own_ref, other_ref, *refs):
    inputs = NL * NX
    parts, outs = refs[:inputs], refs[inputs : inputs + NH * NY]
    panel, sems = refs[inputs + NH * NY :]
    members, window, _, _, size = panel.shape
    half = own_ref.shape[1] // size
    core, group, x, l, h, y = (where[i] for i in range(1, 7))
    step = pl.program_id(0)
    tile = group * window + lax.rem(h + step // NY, NH) * NY + lax.rem(y + step, NY)

    @pl.when(step == 0)
    def _():
        copies = []
        for side in range(NL):
            for hop, shift in enumerate(RING):
                source = lax.rem(x + shift, NX) * NL + lax.rem(l + side, NL)
                i = side * NX + hop
                copies.append(pltpu.make_async_copy(parts[i], panel.at[:, :, source], sems.at[i]))
        for copy in copies:
            copy.start()
        for copy in copies:
            copy.wait()

    for k in range(members):
        cols = slice(k * size, (k + 1) * size)
        wanted = place[core * members + k, tile] >= 0

        def store(values):
            for j, out in enumerate(outs):

                @pl.when(step == j)
                def _():
                    out[:, cols] = values

        @pl.when(wanted)
        def _():
            first = panel[k, pl.ds(core * half, half)].reshape(half * size, size)
            second = panel[k, pl.ds((1 - core) * half, half)].reshape(half * size, size)
            values = jnp.dot(own_ref[...], first, preferred_element_type=F32)
            values += jnp.dot(other_ref[...], second, preferred_element_type=F32)
            level = level_of(jnp.max(jnp.abs(values), axis=0, keepdims=True))
            tail = jnp.broadcast_to(level, (16, size)).astype(jnp.int32).astype(I16)
            store(jnp.concatenate([code(values, level), tail], axis=0))

        @pl.when(jnp.logical_not(wanted))
        def _():
            store(jnp.zeros((size + 16, size), I16))


def diagonal_kernel(place, where, *refs):
    count = NH * NY
    coded, parts, (d_ref, block) = refs[:count], refs[count : 2 * count], refs[2 * count :]
    _, members, _, size = parts[0].shape
    core, group, h, y = where[1], where[2], where[5], where[6]
    block[...] = jnp.zeros_like(block)
    for side in range(NH):
        for hop, shift in enumerate(RING):
            tile = lax.rem(h + side, NH) * NY + lax.rem(y + shift, NY)
            q_ref, ref = coded[side * NY + shift], parts[side * NY + hop]
            for k in range(members):
                cols = slice(k * size, (k + 1) * size)

                @pl.when(place[core * members + k, group * count + tile] >= 0)
                def _():
                    own = ref[:, k].reshape(size, size)
                    rest = plain(q_ref[:size, cols])
                    high = rest.astype(BF16)
                    low = (rest - high.astype(F32)).astype(BF16)
                    total = sum(
                        lax.dot_general(
                            own, term, (((0,), (0,)), ((), ())), preferred_element_type=F32
                        )
                        for term in (high, low)
                    )
                    block[:, cols] -= total * scale_of(plain(q_ref[size : size + 16, cols])[:1])

    values = block[...]
    level = level_of(jnp.max(jnp.abs(values), keepdims=True))
    width = values.shape[1] // 2
    for i in range(2):
        d_ref[i, :, :width] = code(values[:, i * width : (i + 1) * width], level)
        d_ref[i, :, width:] = jnp.broadcast_to(level, (size, LANES)).astype(jnp.int32).astype(I16)


def finish_kernel(place, where, *refs):
    parts, (u_ref, swap_ref) = refs[:-2], refs[-2:]
    sources = len(parts)
    slab, width = u_ref.shape
    size = 2 * slab
    members = width // size
    chip, core, group = where[0], where[1], where[2]
    mine = group * sources + chip
    for k in range(members):
        cols = slice(k * size, (k + 1) * size)
        total = jnp.zeros((size, size), F32)
        for ref in parts:
            scale = scale_of(plain(ref[size : size + 16, cols])[:1])
            total += plain(ref[:size, cols]) * scale
        keep = place[core * members + k, mine] >= 0
        rounded = jnp.where(keep, -total, jnp.zeros_like(total)).astype(BF16)
        first = core == 0
        u_ref[:, cols] = jnp.where(first, rounded[:slab], rounded[slab:])
        swap_ref[:, cols] = jnp.where(first, rounded[slab:], rounded[:slab])


def piece_kernel(q_ref, o_ref):
    width = q_ref.shape[2] - LANES
    scale = scale_of(plain(q_ref[:, :, width:]))
    sums = [
        jnp.sum(plain(q_ref[:, :, i : i + LANES]) * scale, axis=0) for i in range(0, width, LANES)
    ]
    values = jnp.concatenate(sums, axis=1)
    level = level_of(jnp.max(jnp.abs(values), keepdims=True))
    coded = jnp.concatenate(
        [
            code(values, level),
            jnp.broadcast_to(level, (values.shape[0], LANES)).astype(jnp.int32).astype(I16),
        ],
        axis=1,
    )
    for j in range(o_ref.shape[0]):
        o_ref[j] = coded


def total_kernel(q_ref, inverse_ref, o_ref):
    pieces, cores, depth, _ = q_ref.shape
    supers, size, _ = inverse_ref.shape
    width = q_ref.shape[3] - LANES
    count = pieces // 2
    for c in range(cores):
        for i in range(2):
            rows = slice(i * count, (i + 1) * count)
            scale = scale_of(plain(q_ref[rows, c, :, width:]))
            for t in range(width // LANES):
                lane = (i * width + t * LANES) % size
                k = c * (supers // cores) + (i * width + t * LANES) // size
                values = plain(q_ref[rows, c, :, t * LANES : (t + 1) * LANES]) * scale
                values = values.reshape(count * depth, LANES)
                o_ref[k, :, lane : lane + LANES] = (
                    inverse_ref[k, :, lane : lane + LANES] - values
                )


def spread(own, axis, up):
    below = lax.ppermute(own, axis, UP)
    above = lax.ppermute(own, axis, DOWN)
    far = lax.ppermute(below, axis, UP) if up else lax.ppermute(above, axis, DOWN)
    return [own, below, above, far]


RING = (0, 3, 1, 2)


def update(ancestor_inv, lfactor, struct, validity, diag_inverse):
    rows, cols = ancestor_inv.shape
    entries, size, supers, _ = lfactor.shape
    groups = NX * NL
    chips = NH * NY
    part = size // groups
    members = supers // NC
    width = members * size
    group = lax.axis_index(XL)
    chip = lax.axis_index(HY)
    core = lax.axis_index("c")
    listed = struct.shape[1]
    tiles = rows * groups // size
    window = tiles // chips
    smem = pl.BlockSpec(memory_space=pltpu.SMEM)
    vmem = pl.BlockSpec(memory_space=pltpu.VMEM)

    other = lax.ppermute(ancestor_inv, "c", CORE_SWAP)

    hits = (struct[:, :, None] == jnp.arange(tiles, dtype=jnp.int32)) & (validity[:, :, None] > 0)
    position = jnp.arange(listed, dtype=jnp.int32)[None, :, None]
    place = jnp.max(jnp.where(hits, position, -1), axis=1)
    where = jnp.stack([chip, core, group] + [lax.axis_index(a) for a in ("x", "l", "h", "y")])

    share = jnp.transpose(lfactor, (0, 2, 1, 3))
    share = lax.dynamic_slice_in_dim(share, group * part, part, 2)
    share = share.reshape(entries, NC, members, part, size)
    share = jnp.transpose(share, (1, 0, 2, 3, 4))
    share = jnp.broadcast_to(share[None], (chips,) + share.shape)
    share = share.reshape((chips * NC,) + share.shape[2:])
    share = lax.all_to_all(share, ("h", "y", "c"), split_axis=0, concat_axis=0, tiled=True)
    share = share.reshape(listed, members, part, size)

    block = jax.ShapeDtypeStruct((members, window, part, size), BF16)
    near, own = pl.pallas_call(
        pick_kernel,
        out_shape=[block, jax.ShapeDtypeStruct((groups, members, part, size), BF16)],
        in_specs=[smem, smem, vmem],
        out_specs=[vmem] * 2,
        name="pick",
    )(place, where, share)
    across = lax.ppermute(near, "l", CORE_SWAP)
    window_parts = spread(near, "x", True)
    window_parts += spread(across, "x", False)
    own = lax.all_to_all(own, XL, split_axis=0, concat_axis=0, tiled=True)
    across = lax.ppermute(own, "h", CORE_SWAP)
    row_parts = spread(own, "y", True)
    row_parts += spread(across, "y", False)

    def row_tile(j, _, where):
        return lax.rem(where[5] + j // NY, NH) * NY + lax.rem(where[6] + j, NY), 0

    coded = pl.pallas_call(
        product_kernel,
        out_shape=[jax.ShapeDtypeStruct((size + 16, width), I16)] * chips,
        grid_spec=pltpu.PrefetchScalarGridSpec(
            num_scalar_prefetch=2,
            grid=(chips,),
            in_specs=[pl.BlockSpec((size, cols), row_tile)] * 2
            + [pl.BlockSpec(memory_space=pl.ANY)] * len(window_parts),
            out_specs=[vmem] * chips,
            scratch_shapes=[
                pltpu.VMEM((members, window, groups, part, size), BF16),
                pltpu.SemaphoreType.DMA((len(window_parts),)),
            ],
        ),
        name="product",
    )(place, where, ancestor_inv, other, *window_parts)
    pieces = groups * chips
    depth = 2 * size // pieces
    reach = width // 2 + LANES
    diag = pl.pallas_call(
        diagonal_kernel,
        out_shape=jax.ShapeDtypeStruct((2, size, reach), I16),
        in_specs=[smem, smem] + [vmem] * (chips + len(row_parts)),
        out_specs=vmem,
        scratch_shapes=[pltpu.VMEM((size, width), F32)],
        name="diagonal",
    )(place, where, *coded, *row_parts)

    sums = [coded[0]]
    for shifts in ((6, 5, 7), (2, 4, 1, 3)):
        for j in shifts:
            to = [
                (h * NY + y, (h + j // NY) % NH * NY + (y + j) % NY)
                for h in range(NH)
                for y in range(NY)
            ]
            sums.append(lax.ppermute(coded[j], HY, to))
    slab = jax.ShapeDtypeStruct((size // NC, width), BF16)
    mine, theirs = pl.pallas_call(
        finish_kernel,
        out_shape=[slab, slab],
        in_specs=[smem, smem] + [vmem] * len(sums),
        out_specs=[vmem] * 2,
        name="finish",
    )(place, where, *sums)

    theirs = lax.ppermute(theirs, "c", CORE_SWAP)
    column_block = jnp.where(
        core == 0,
        jnp.concatenate([mine, theirs], axis=1),
        jnp.concatenate([theirs, mine], axis=1),
    )

    diag = diag.reshape(pieces, depth, reach)
    diag = lax.all_to_all(diag, CHIPS, split_axis=0, concat_axis=0, tiled=True)
    piece = pl.pallas_call(
        piece_kernel,
        out_shape=jax.ShapeDtypeStruct((pieces * NC, depth, reach), I16),
        in_specs=[vmem],
        out_specs=vmem,
        name="piece",
    )(diag)
    whole = lax.all_to_all(piece, CHIPS + ("c",), split_axis=0, concat_axis=0, tiled=True)
    diagonal = pl.pallas_call(
        total_kernel,
        out_shape=jax.ShapeDtypeStruct(diag_inverse.shape, F32),
        in_specs=[vmem, vmem],
        out_specs=vmem,
        name="total",
    )(whole.reshape(pieces, NC, depth, reach), diag_inverse)
    return column_block, diagonal


def solution(mesh):
    fine = Mesh(mesh.devices.reshape(NX, NL, NH, NY, NC), ("x", "l", "h", "y", "c"))
    return jax.shard_map(
        update,
        mesh=fine,
        in_specs=(P(XL, ("h", "y", "c")), P(("h", "y", "c")), P(), P(), P()),
        out_specs=(P(("x", "l", "h", "y", "c")), P()),
        check_vma=False,
    )
```

```python
import jax
import jax.numpy as jnp
from jax import lax
from jax.experimental import pallas as pl
from jax.experimental.pallas import tpu as pltpu
from jax.sharding import Mesh, PartitionSpec as P


BF16 = jnp.bfloat16
F32 = jnp.float32
I16 = jnp.int16
NX, NL, NH, NY, NC = 4, 2, 2, 4, 2
XL = ("x", "l")
HY = ("h", "y")
CHIPS = XL + HY
CORE_SWAP = [(0, 1), (1, 0)]
UP = [(i, (i + 1) % NX) for i in range(NX)]
DOWN = [(i, (i - 1) % NX) for i in range(NX)]
LEVELS = 32000.0
LOWEST = -100.0
LANES = 128


def level_of(top):
    return jnp.maximum(jnp.ceil(jnp.log2(jnp.maximum(top, 1e-37)) + 0.01), LOWEST)


def code(values, level):
    return jnp.round(values * (jnp.exp2(-level) * LEVELS)).astype(jnp.int32).astype(I16)


def plain(coded):
    return coded.astype(jnp.int32).astype(F32)


def scale_of(level):
    return jnp.exp2(level) * (1.0 / LEVELS)


def pick_kernel(place, where, x_ref, window_ref, own_ref):
    members, window = window_ref.shape[:2]
    groups = own_ref.shape[0]
    chip, core = where[0], where[1]
    for k in range(members):

        def tile(t):
            p = place[core * members + k, t]
            block = x_ref[jnp.maximum(p, 0), k]
            return jnp.where(p >= 0, block, jnp.zeros_like(block))

        for s in range(window):
            window_ref[k, s] = tile(chip * window + s)
        for g in range(groups):
            own_ref[g, k] = tile(g * window + chip)


def product_kernel(place, where, own_ref, other_ref, *refs):
    inputs = NL * NX
    parts, outs = refs[:inputs], refs[inputs : inputs + NH * NY]
    panel, sems = refs[inputs + NH * NY :]
    members, window, _, _, size = panel.shape
    half = own_ref.shape[1] // size
    core, group, x, l, h, y = (where[i] for i in range(1, 7))
    step = pl.program_id(0)
    tile = group * window + lax.rem(h + step // NY, NH) * NY + lax.rem(y + step, NY)

    @pl.when(step == 0)
    def _():
        copies = []
        for side in range(NL):
            for hop, shift in enumerate(RING):
                source = lax.rem(x + shift, NX) * NL + lax.rem(l + side, NL)
                i = side * NX + hop
                copies.append(pltpu.make_async_copy(parts[i], panel.at[:, :, source], sems.at[i]))
        for copy in copies:
            copy.start()
        for copy in copies:
            copy.wait()

    for k in range(members):
        cols = slice(k * size, (k + 1) * size)
        wanted = place[core * members + k, tile] >= 0

        def store(values):
            for j, out in enumerate(outs):

                @pl.when(step == j)
                def _():
                    out[:, cols] = values

        @pl.when(wanted)
        def _():
            first = panel[k, pl.ds(core * half, half)].reshape(half * size, size)
            second = panel[k, pl.ds((1 - core) * half, half)].reshape(half * size, size)
            values = jnp.dot(own_ref[...], first, preferred_element_type=F32)
            values += jnp.dot(other_ref[...], second, preferred_element_type=F32)
            level = level_of(jnp.max(jnp.abs(values), axis=0, keepdims=True))
            tail = jnp.broadcast_to(level, (16, size)).astype(jnp.int32).astype(I16)
            store(jnp.concatenate([code(values, level), tail], axis=0))

        @pl.when(jnp.logical_not(wanted))
        def _():
            store(jnp.zeros((size + 16, size), I16))


def diagonal_kernel(place, where, *refs):
    count = NH * NY
    coded, parts, (d_ref, block) = refs[:count], refs[count : 2 * count], refs[2 * count :]
    _, members, _, size = parts[0].shape
    core, group, h, y = where[1], where[2], where[5], where[6]
    block[...] = jnp.zeros_like(block)
    for side in range(NH):
        for hop, shift in enumerate(RING):
            tile = lax.rem(h + side, NH) * NY + lax.rem(y + shift, NY)
            q_ref, ref = coded[side * NY + shift], parts[side * NY + hop]
            for k in range(members):
                cols = slice(k * size, (k + 1) * size)

                @pl.when(place[core * members + k, group * count + tile] >= 0)
                def _():
                    own = ref[:, k].reshape(size, size)
                    rest = plain(q_ref[:size, cols])
                    high = rest.astype(BF16)
                    low = (rest - high.astype(F32)).astype(BF16)
                    total = sum(
                        lax.dot_general(
                            own, term, (((0,), (0,)), ((), ())), preferred_element_type=F32
                        )
                        for term in (high, low)
                    )
                    block[:, cols] -= total * scale_of(plain(q_ref[size : size + 16, cols])[:1])

    values = block[...]
    level = level_of(jnp.max(jnp.abs(values), keepdims=True))
    width = values.shape[1] // 2
    for i in range(2):
        d_ref[i, :, :width] = code(values[:, i * width : (i + 1) * width], level)
        d_ref[i, :, width:] = jnp.broadcast_to(level, (size, LANES)).astype(jnp.int32).astype(I16)


def finish_kernel(place, where, *refs):
    parts, (u_ref, swap_ref) = refs[:-2], refs[-2:]
    sources = len(parts)
    slab, width = u_ref.shape
    size = 2 * slab
    members = width // size
    chip, core, group = where[0], where[1], where[2]
    mine = group * sources + chip
    for k in range(members):
        cols = slice(k * size, (k + 1) * size)
        total = jnp.zeros((size, size), F32)
        for ref in parts:
            scale = scale_of(plain(ref[size : size + 16, cols])[:1])
            total += plain(ref[:size, cols]) * scale
        keep = place[core * members + k, mine] >= 0
        rounded = jnp.where(keep, -total, jnp.zeros_like(total)).astype(BF16)
        first = core == 0
        u_ref[:, cols] = jnp.where(first, rounded[:slab], rounded[slab:])
        swap_ref[:, cols] = jnp.where(first, rounded[slab:], rounded[:slab])


def piece_kernel(q_ref, o_ref):
    width = q_ref.shape[2] - LANES
    scale = scale_of(plain(q_ref[:, :, width:]))
    sums = [
        jnp.sum(plain(q_ref[:, :, i : i + LANES]) * scale, axis=0) for i in range(0, width, LANES)
    ]
    values = jnp.concatenate(sums, axis=1)
    level = level_of(jnp.max(jnp.abs(values), keepdims=True))
    coded = jnp.concatenate(
        [
            code(values, level),
            jnp.broadcast_to(level, (values.shape[0], LANES)).astype(jnp.int32).astype(I16),
        ],
        axis=1,
    )
    for j in range(o_ref.shape[0]):
        o_ref[j] = coded


def total_kernel(q_ref, inverse_ref, o_ref):
    pieces, cores, depth, _ = q_ref.shape
    supers, size, _ = inverse_ref.shape
    width = q_ref.shape[3] - LANES
    count = pieces // 2
    for c in range(cores):
        for i in range(2):
            rows = slice(i * count, (i + 1) * count)
            scale = scale_of(plain(q_ref[rows, c, :, width:]))
            for t in range(width // LANES):
                lane = (i * width + t * LANES) % size
                k = c * (supers // cores) + (i * width + t * LANES) // size
                values = plain(q_ref[rows, c, :, t * LANES : (t + 1) * LANES]) * scale
                values = values.reshape(count * depth, LANES)
                o_ref[k, :, lane : lane + LANES] = (
                    inverse_ref[k, :, lane : lane + LANES] - values
                )


def spread(own, axis, up):
    below = lax.ppermute(own, axis, UP)
    above = lax.ppermute(own, axis, DOWN)
    far = lax.ppermute(below, axis, UP) if up else lax.ppermute(above, axis, DOWN)
    return [own, below, above, far]


RING = (0, 3, 1, 2)


def update(ancestor_inv, lfactor, struct, validity, diag_inverse):
    rows, cols = ancestor_inv.shape
    entries, size, supers, _ = lfactor.shape
    groups = NX * NL
    chips = NH * NY
    part = size // groups
    members = supers // NC
    width = members * size
    group = lax.axis_index(XL)
    chip = lax.axis_index(HY)
    core = lax.axis_index("c")
    listed = struct.shape[1]
    tiles = rows * groups // size
    window = tiles // chips
    smem = pl.BlockSpec(memory_space=pltpu.SMEM)
    vmem = pl.BlockSpec(memory_space=pltpu.VMEM)

    other = lax.ppermute(ancestor_inv, "c", CORE_SWAP)

    hits = (struct[:, :, None] == jnp.arange(tiles, dtype=jnp.int32)) & (validity[:, :, None] > 0)
    position = jnp.arange(listed, dtype=jnp.int32)[None, :, None]
    place = jnp.max(jnp.where(hits, position, -1), axis=1)
    where = jnp.stack([chip, core, group] + [lax.axis_index(a) for a in ("x", "l", "h", "y")])

    share = jnp.transpose(lfactor, (0, 2, 1, 3))
    share = lax.dynamic_slice_in_dim(share, group * part, part, 2)
    share = share.reshape(entries, NC, members, part, size)
    share = jnp.transpose(share, (1, 0, 2, 3, 4))
    share = jnp.broadcast_to(share[None], (chips,) + share.shape)
    share = share.reshape((chips * NC,) + share.shape[2:])
    share = lax.all_to_all(share, ("h", "y", "c"), split_axis=0, concat_axis=0, tiled=True)
    share = share.reshape(listed, members, part, size)

    block = jax.ShapeDtypeStruct((members, window, part, size), BF16)
    near, own = pl.pallas_call(
        pick_kernel,
        out_shape=[block, jax.ShapeDtypeStruct((groups, members, part, size), BF16)],
        in_specs=[smem, smem, vmem],
        out_specs=[vmem] * 2,
        compiler_params=pltpu.CompilerParams(vmem_limit_bytes=8 << 20),
        name="pick",
    )(place, where, share)
    across = lax.ppermute(near, "l", CORE_SWAP)
    window_parts = spread(near, "x", True)
    window_parts += spread(across, "x", False)
    own = lax.all_to_all(own, XL, split_axis=0, concat_axis=0, tiled=True)
    across = lax.ppermute(own, "h", CORE_SWAP)
    row_parts = spread(own, "y", True)
    row_parts += spread(across, "y", False)

    def row_tile(j, _, where):
        return lax.rem(where[5] + j // NY, NH) * NY + lax.rem(where[6] + j, NY), 0

    coded = pl.pallas_call(
        product_kernel,
        out_shape=[jax.ShapeDtypeStruct((size + 16, width), I16)] * chips,
        grid_spec=pltpu.PrefetchScalarGridSpec(
            num_scalar_prefetch=2,
            grid=(chips,),
            in_specs=[pl.BlockSpec((size, cols), row_tile)] * 2
            + [pl.BlockSpec(memory_space=pl.ANY)] * len(window_parts),
            out_specs=[vmem] * chips,
            scratch_shapes=[
                pltpu.VMEM((members, window, groups, part, size), BF16),
                pltpu.SemaphoreType.DMA((len(window_parts),)),
            ],
        ),
        compiler_params=pltpu.CompilerParams(vmem_limit_bytes=20 << 20),
        name="product",
    )(place, where, ancestor_inv, other, *window_parts)
    pieces = groups * chips
    depth = 2 * size // pieces
    reach = width // 2 + LANES
    diag = pl.pallas_call(
        diagonal_kernel,
        out_shape=jax.ShapeDtypeStruct((2, size, reach), I16),
        in_specs=[smem, smem] + [vmem] * (chips + len(row_parts)),
        out_specs=vmem,
        scratch_shapes=[pltpu.VMEM((size, width), F32)],
        compiler_params=pltpu.CompilerParams(vmem_limit_bytes=16 << 20),
        name="diagonal",
    )(place, where, *coded, *row_parts)

    sums = [coded[0]]
    for shifts in ((6, 5, 7), (2, 4, 1, 3)):
        for j in shifts:
            to = [
                (h * NY + y, (h + j // NY) % NH * NY + (y + j) % NY)
                for h in range(NH)
                for y in range(NY)
            ]
            sums.append(lax.ppermute(coded[j], HY, to))
    slab = jax.ShapeDtypeStruct((size // NC, width), BF16)
    mine, theirs = pl.pallas_call(
        finish_kernel,
        out_shape=[slab, slab],
        in_specs=[smem, smem] + [vmem] * len(sums),
        out_specs=[vmem] * 2,
        compiler_params=pltpu.CompilerParams(vmem_limit_bytes=12 << 20),
        name="finish",
    )(place, where, *sums)

    theirs = lax.ppermute(theirs, "c", CORE_SWAP)
    column_block = jnp.where(
        core == 0,
        jnp.concatenate([mine, theirs], axis=1),
        jnp.concatenate([theirs, mine], axis=1),
    )

    diag = diag.reshape(pieces, depth, reach)
    diag = lax.all_to_all(diag, CHIPS, split_axis=0, concat_axis=0, tiled=True)
    piece = pl.pallas_call(
        piece_kernel,
        out_shape=jax.ShapeDtypeStruct((pieces * NC, depth, reach), I16),
        in_specs=[vmem],
        out_specs=vmem,
        compiler_params=pltpu.CompilerParams(vmem_limit_bytes=6 << 20),
        name="piece",
    )(diag)
    whole = lax.all_to_all(piece, CHIPS + ("c",), split_axis=0, concat_axis=0, tiled=True)
    diagonal = pl.pallas_call(
        total_kernel,
        out_shape=jax.ShapeDtypeStruct(diag_inverse.shape, F32),
        in_specs=[vmem, vmem],
        out_specs=vmem,
        compiler_params=pltpu.CompilerParams(vmem_limit_bytes=12 << 20),
        name="total",
    )(whole.reshape(pieces, NC, depth, reach), diag_inverse)
    return column_block, diagonal


def solution(mesh):
    fine = Mesh(mesh.devices.reshape(NX, NL, NH, NY, NC), ("x", "l", "h", "y", "c"))
    return jax.shard_map(
        update,
        mesh=fine,
        in_specs=(P(XL, ("h", "y", "c")), P(("h", "y", "c")), P(), P(), P()),
        out_specs=(P(("x", "l", "h", "y", "c")), P()),
        check_vma=False,
    )
```

```python
import jax
import jax.numpy as jnp
from jax import lax
from jax.experimental import pallas as pl
from jax.experimental.pallas import tpu as pltpu
from jax.sharding import Mesh, PartitionSpec as P


BF16 = jnp.bfloat16
F32 = jnp.float32
I16 = jnp.int16
NX, NL, NH, NY, NC = 4, 2, 2, 4, 2
XL = ("x", "l")
HY = ("h", "y")
CHIPS = XL + HY
CORE_SWAP = [(0, 1), (1, 0)]
UP = [(i, (i + 1) % NX) for i in range(NX)]
DOWN = [(i, (i - 1) % NX) for i in range(NX)]
LEVELS = 32000.0
LOWEST = -100.0
LANES = 128


def level_of(top):
    return jnp.maximum(jnp.ceil(jnp.log2(jnp.maximum(top, 1e-37)) + 0.01), LOWEST)


def code(values, level):
    return jnp.round(values * (jnp.exp2(-level) * LEVELS)).astype(jnp.int32).astype(I16)


def plain(coded):
    return coded.astype(jnp.int32).astype(F32)


def scale_of(level):
    return jnp.exp2(level) * (1.0 / LEVELS)


def share_kernel(where, l_ref, o_ref, buffer, sem):
    part = o_ref.shape[3]
    copy = pltpu.make_async_copy(
        l_ref.at[:, :, pl.ds(pl.multiple_of(where[2] * part, part), part)], buffer, sem
    )
    copy.start()
    copy.wait()
    members = o_ref.shape[2]
    for i in range(o_ref.shape[0]):
        core = i % NC
        o_ref[i] = buffer[:, core * members : (core + 1) * members]


def stage_kernel(where, own_ref, other_ref, o_ref, sems):
    core = where[1]
    copies = [
        pltpu.make_async_copy(own_ref, o_ref.at[core], sems.at[0]),
        pltpu.make_async_copy(other_ref, o_ref.at[1 - core], sems.at[1]),
    ]
    for copy in copies:
        copy.start()
    for copy in copies:
        copy.wait()


def pick_kernel(place, where, x_ref, window_ref, own_ref):
    members, window = window_ref.shape[:2]
    groups = own_ref.shape[0]
    chip, core = where[0], where[1]
    for k in range(members):

        def tile(t):
            p = place[core * members + k, t]
            block = x_ref[jnp.maximum(p, 0), k]
            return jnp.where(p >= 0, block, jnp.zeros_like(block))

        for s in range(window):
            window_ref[k, s] = tile(chip * window + s)
        for g in range(groups):
            own_ref[g, k] = tile(g * window + chip)


def product_kernel(place, where, a_ref, *refs):
    inputs = NL * NX
    parts, outs = refs[:inputs], refs[inputs : inputs + NH * NY]
    panel, order, sems = refs[inputs + NH * NY :]
    members, window, _, _, size = panel.shape
    half = window // NC
    chip, core, group, x, l, h, y = (where[i] for i in range(7))
    step = pl.program_id(0)
    tile = group * window + lax.rem(h + step // NY, NH) * NY + lax.rem(y + step, NY)

    @pl.when(step == 0)
    def _():
        copies = []
        for side in range(NL):
            for hop, shift in enumerate(RING):
                source = lax.rem(x + shift, NX) * NL + lax.rem(l + side, NL)
                i = side * NX + hop
                copies.append(pltpu.make_async_copy(parts[i], panel.at[:, :, source], sems.at[i]))
        for copy in copies:
            copy.start()
        for k in range(members):
            listed = [place[core * members + k, chip * window + s] >= 0 for s in range(window)]
            count = sum(jnp.where(f, 1, 0) for f in listed)
            order[k, window] = count
            front, back = jnp.int32(0), count
            for s in range(window):
                order[k, jnp.where(listed[s], front, back)] = s
                front = front + jnp.where(listed[s], 1, 0)
                back = back + jnp.where(listed[s], 0, 1)
        for copy in copies:
            copy.wait()

    for k in range(members):
        cols = slice(k * size, (k + 1) * size)
        wanted = place[core * members + k, tile] >= 0
        few = order[k, window] <= half

        def store(values):
            for j, out in enumerate(outs):

                @pl.when(step == j)
                def _():
                    out[:, cols] = values

        def finish(tiles):
            values = jnp.zeros((size, size), F32)
            for s in tiles:
                start = pl.multiple_of(lax.rem(s, half) * size, size)
                left = a_ref[lax.div(s, half), :, pl.ds(start, size)]
                values += jnp.dot(left, panel[k, s].reshape(size, size), preferred_element_type=F32)
            level = level_of(jnp.max(jnp.abs(values), axis=0, keepdims=True))
            tail = jnp.broadcast_to(level, (16, size)).astype(jnp.int32).astype(I16)
            store(jnp.concatenate([code(values, level), tail], axis=0))

        @pl.when(jnp.logical_and(wanted, few))
        def _():
            finish([order[k, i] for i in range(half)])

        @pl.when(jnp.logical_and(wanted, jnp.logical_not(few)))
        def _():
            finish([jnp.int32(s) for s in range(window)])

        @pl.when(jnp.logical_not(wanted))
        def _():
            store(jnp.zeros((size + 16, size), I16))


def diagonal_kernel(place, where, *refs):
    count = NH * NY
    coded, parts, (d_ref, block) = refs[:count], refs[count : 2 * count], refs[2 * count :]
    _, members, _, size = parts[0].shape
    core, group, h, y = where[1], where[2], where[5], where[6]
    block[...] = jnp.zeros_like(block)
    for side in range(NH):
        for hop, shift in enumerate(RING):
            tile = lax.rem(h + side, NH) * NY + lax.rem(y + shift, NY)
            q_ref, ref = coded[side * NY + shift], parts[side * NY + hop]
            for k in range(members):
                cols = slice(k * size, (k + 1) * size)

                @pl.when(place[core * members + k, group * count + tile] >= 0)
                def _():
                    own = ref[:, k].reshape(size, size)
                    rest = plain(q_ref[:size, cols])
                    high = rest.astype(BF16)
                    low = (rest - high.astype(F32)).astype(BF16)
                    total = sum(
                        lax.dot_general(
                            own, term, (((0,), (0,)), ((), ())), preferred_element_type=F32
                        )
                        for term in (high, low)
                    )
                    block[:, cols] -= total * scale_of(plain(q_ref[size : size + 16, cols])[:1])

    values = block[...]
    level = level_of(jnp.max(jnp.abs(values), keepdims=True))
    width = values.shape[1] // 2
    for i in range(2):
        d_ref[i, :, :width] = code(values[:, i * width : (i + 1) * width], level)
        d_ref[i, :, width:] = jnp.broadcast_to(level, (size, LANES)).astype(jnp.int32).astype(I16)


def finish_kernel(place, where, *refs):
    parts, (u_ref, swap_ref) = refs[:-2], refs[-2:]
    sources = len(parts)
    slab, width = u_ref.shape
    size = 2 * slab
    members = width // size
    chip, core, group = where[0], where[1], where[2]
    mine = group * sources + chip
    for k in range(members):
        cols = slice(k * size, (k + 1) * size)
        total = jnp.zeros((size, size), F32)
        for ref in parts:
            scale = scale_of(plain(ref[size : size + 16, cols])[:1])
            total += plain(ref[:size, cols]) * scale
        keep = place[core * members + k, mine] >= 0
        rounded = jnp.where(keep, -total, jnp.zeros_like(total)).astype(BF16)
        first = core == 0
        u_ref[:, cols] = jnp.where(first, rounded[:slab], rounded[slab:])
        swap_ref[:, cols] = jnp.where(first, rounded[slab:], rounded[:slab])


def piece_kernel(q_ref, inverse_ref, o_ref):
    width = q_ref.shape[2] - LANES
    scale = scale_of(plain(q_ref[:, :, width:]))
    sums = [
        jnp.sum(plain(q_ref[:, :, i : i + LANES]) * scale, axis=0) for i in range(0, width, LANES)
    ]
    values = inverse_ref[...] - jnp.concatenate(sums, axis=1)
    level = level_of(jnp.max(jnp.abs(values), keepdims=True))
    coded = jnp.concatenate(
        [
            code(values, level),
            jnp.broadcast_to(level, (values.shape[0], LANES)).astype(jnp.int32).astype(I16),
        ],
        axis=1,
    )
    for j in range(o_ref.shape[0]):
        o_ref[j] = coded


def total_kernel(q_ref, o_ref):
    pieces, cores, depth, reach = q_ref.shape
    supers, size, _ = o_ref.shape
    width = reach - LANES
    count = pieces // 2
    for c in range(cores):
        for i in range(2):
            rows = slice(i * count, (i + 1) * count)
            scale = scale_of(plain(q_ref[rows, c, :, width:]))
            for t in range(width // LANES):
                lane = (i * width + t * LANES) % size
                k = c * (supers // cores) + (i * width + t * LANES) // size
                values = plain(q_ref[rows, c, :, t * LANES : (t + 1) * LANES]) * scale
                o_ref[k, :, lane : lane + LANES] = values.reshape(count * depth, LANES)


def spread(own, axis, up):
    below = lax.ppermute(own, axis, UP)
    above = lax.ppermute(own, axis, DOWN)
    far = lax.ppermute(below, axis, UP) if up else lax.ppermute(above, axis, DOWN)
    return [own, below, above, far]


RING = (0, 3, 1, 2)


def update(ancestor_inv, lfactor, struct, validity, diag_inverse):
    rows, cols = ancestor_inv.shape
    entries, size, supers, _ = lfactor.shape
    groups = NX * NL
    chips = NH * NY
    part = size // groups
    members = supers // NC
    width = members * size
    group = lax.axis_index(XL)
    chip = lax.axis_index(HY)
    core = lax.axis_index("c")
    listed = struct.shape[1]
    tiles = rows * groups // size
    window = tiles // chips
    smem = pl.BlockSpec(memory_space=pltpu.SMEM)
    vmem = pl.BlockSpec(memory_space=pltpu.VMEM)

    other = lax.ppermute(ancestor_inv, "c", CORE_SWAP)

    hits = (struct[:, :, None] == jnp.arange(tiles, dtype=jnp.int32)) & (validity[:, :, None] > 0)
    position = jnp.arange(listed, dtype=jnp.int32)[None, :, None]
    place = jnp.max(jnp.where(hits, position, -1), axis=1)
    where = jnp.stack([chip, core, group] + [lax.axis_index(a) for a in ("x", "l", "h", "y")])

    share = pl.pallas_call(
        share_kernel,
        out_shape=jax.ShapeDtypeStruct((chips * NC, entries, members, part, size), BF16),
        in_specs=[smem, pl.BlockSpec(memory_space=pltpu.HBM)],
        out_specs=vmem,
        scratch_shapes=[
            pltpu.VMEM((entries, supers, part, size), BF16),
            pltpu.SemaphoreType.DMA,
        ],
        name="share",
    )(where, jnp.transpose(lfactor, (0, 2, 1, 3)))
    share = lax.all_to_all(share, ("h", "y", "c"), split_axis=0, concat_axis=0, tiled=True)
    share = share.reshape(listed, members, part, size)

    block = jax.ShapeDtypeStruct((members, window, part, size), BF16)
    near, own = pl.pallas_call(
        pick_kernel,
        out_shape=[block, jax.ShapeDtypeStruct((groups, members, part, size), BF16)],
        in_specs=[smem, smem, vmem],
        out_specs=[vmem] * 2,
        compiler_params=pltpu.CompilerParams(vmem_limit_bytes=8 << 20),
        name="pick",
    )(place, where, share)
    across = lax.ppermute(near, "l", CORE_SWAP)
    window_parts = spread(near, "x", True)
    window_parts += spread(across, "x", False)
    own = lax.all_to_all(own, XL, split_axis=0, concat_axis=0, tiled=True)
    across = lax.ppermute(own, "h", CORE_SWAP)
    row_parts = spread(own, "y", True)
    row_parts += spread(across, "y", False)

    staged = pl.pallas_call(
        stage_kernel,
        out_shape=jax.ShapeDtypeStruct((NC, rows, cols), BF16),
        in_specs=[smem, pl.BlockSpec(memory_space=pl.ANY), pl.BlockSpec(memory_space=pl.ANY)],
        out_specs=pl.BlockSpec(memory_space=pl.ANY),
        scratch_shapes=[pltpu.SemaphoreType.DMA((2,))],
        compiler_params=pltpu.CompilerParams(vmem_limit_bytes=1 << 20),
        name="stage",
    )(where, ancestor_inv, other)

    def row_tile(j, _, where):
        return 0, lax.rem(where[5] + j // NY, NH) * NY + lax.rem(where[6] + j, NY), 0

    coded = pl.pallas_call(
        product_kernel,
        out_shape=[jax.ShapeDtypeStruct((size + 16, width), I16)] * chips,
        grid_spec=pltpu.PrefetchScalarGridSpec(
            num_scalar_prefetch=2,
            grid=(chips,),
            in_specs=[pl.BlockSpec((NC, size, cols), row_tile)]
            + [pl.BlockSpec(memory_space=pltpu.HBM)] * len(window_parts),
            out_specs=[vmem] * chips,
            scratch_shapes=[
                pltpu.VMEM((members, window, groups, part, size), BF16),
                pltpu.SMEM((members, window + 1), jnp.int32),
                pltpu.SemaphoreType.DMA((len(window_parts),)),
            ],
        ),
        compiler_params=pltpu.CompilerParams(vmem_limit_bytes=20 << 20),
        name="product",
    )(place, where, staged, *window_parts)
    pieces = groups * chips
    depth = 2 * size // pieces
    reach = width // 2 + LANES
    diag = pl.pallas_call(
        diagonal_kernel,
        out_shape=jax.ShapeDtypeStruct((2, size, reach), I16),
        in_specs=[smem, smem] + [vmem] * (chips + len(row_parts)),
        out_specs=vmem,
        scratch_shapes=[pltpu.VMEM((size, width), F32)],
        compiler_params=pltpu.CompilerParams(vmem_limit_bytes=16 << 20),
        name="diagonal",
    )(place, where, *coded, *row_parts)

    sums = [coded[0]]
    for shifts in ((6, 5, 7), (2, 4, 1, 3)):
        for j in shifts:
            to = [
                (h * NY + y, (h + j // NY) % NH * NY + (y + j) % NY)
                for h in range(NH)
                for y in range(NY)
            ]
            sums.append(lax.ppermute(coded[j], HY, to))
    slab = jax.ShapeDtypeStruct((size // NC, width), BF16)
    mine, theirs = pl.pallas_call(
        finish_kernel,
        out_shape=[slab, slab],
        in_specs=[smem, smem] + [vmem] * len(sums),
        out_specs=[vmem] * 2,
        compiler_params=pltpu.CompilerParams(vmem_limit_bytes=12 << 20),
        name="finish",
    )(place, where, *sums)

    theirs = lax.ppermute(theirs, "c", CORE_SWAP)
    column_block = jnp.where(
        core == 0,
        jnp.concatenate([mine, theirs], axis=1),
        jnp.concatenate([theirs, mine], axis=1),
    )

    diag = diag.reshape(pieces, depth, reach)
    diag = lax.all_to_all(diag, CHIPS, split_axis=0, concat_axis=0, tiled=True)
    index = group * chips + chip
    inverse = lax.dynamic_slice(
        diag_inverse,
        (core * members, index % (pieces // 2) * depth, 0),
        (members, depth, size),
    )
    inverse = jnp.transpose(inverse, (1, 0, 2)).reshape(depth, 2, width // 2)
    inverse = lax.dynamic_index_in_dim(inverse, index // (pieces // 2), 1, keepdims=False)
    piece = pl.pallas_call(
        piece_kernel,
        out_shape=jax.ShapeDtypeStruct((pieces * NC, depth, reach), I16),
        in_specs=[vmem, vmem],
        out_specs=vmem,
        compiler_params=pltpu.CompilerParams(vmem_limit_bytes=6 << 20),
        name="piece",
    )(diag, inverse)
    whole = lax.all_to_all(piece, CHIPS + ("c",), split_axis=0, concat_axis=0, tiled=True)
    diagonal = pl.pallas_call(
        total_kernel,
        out_shape=jax.ShapeDtypeStruct(diag_inverse.shape, F32),
        in_specs=[vmem],
        out_specs=vmem,
        compiler_params=pltpu.CompilerParams(vmem_limit_bytes=12 << 20),
        name="total",
    )(whole.reshape(pieces, NC, depth, reach))
    return column_block, diagonal


def solution(mesh):
    fine = Mesh(mesh.devices.reshape(NX, NL, NH, NY, NC), ("x", "l", "h", "y", "c"))
    return jax.shard_map(
        update,
        mesh=fine,
        in_specs=(P(XL, ("h", "y", "c")), P(("h", "y", "c")), P(), P(), P()),
        out_specs=(P(("x", "l", "h", "y", "c")), P()),
        check_vma=False,
    )
```

```python
import jax
import jax.numpy as jnp
from jax import lax
from jax.experimental import pallas as pl
from jax.experimental.pallas import tpu as pltpu
from jax.sharding import Mesh, PartitionSpec as P


BF16 = jnp.bfloat16
F32 = jnp.float32
I16 = jnp.int16
NX, NL, NH, NY, NC = 4, 2, 2, 4, 2
XL = ("x", "l")
HY = ("h", "y")
CORE_SWAP = [(0, 1), (1, 0)]
UP = [(i, (i + 1) % NX) for i in range(NX)]
DOWN = [(i, (i - 1) % NX) for i in range(NX)]
LEVELS = 32000.0
LOWEST = -100.0
LANES = 128


def level_of(top):
    return jnp.maximum(jnp.ceil(jnp.log2(jnp.maximum(top, 1e-37)) + 0.01), LOWEST)


def code(values, level):
    return jnp.round(values * (jnp.exp2(-level) * LEVELS)).astype(jnp.int32).astype(I16)


def plain(coded):
    return coded.astype(jnp.int32).astype(F32)


def scale_of(level):
    return jnp.exp2(level) * (1.0 / LEVELS)


def share_kernel(where, l_ref, o_ref, buffer, sem):
    part = o_ref.shape[3]
    copy = pltpu.make_async_copy(
        l_ref.at[:, :, pl.ds(pl.multiple_of(where[2] * part, part), part)], buffer, sem
    )
    copy.start()
    copy.wait()
    members = o_ref.shape[2]
    for i in range(o_ref.shape[0]):
        core = i % NC
        o_ref[i] = buffer[:, core * members : (core + 1) * members]


def stage_kernel(where, own_ref, other_ref, o_ref, sems):
    core = where[1]
    copies = [
        pltpu.make_async_copy(own_ref, o_ref.at[core], sems.at[0]),
        pltpu.make_async_copy(other_ref, o_ref.at[1 - core], sems.at[1]),
    ]
    for copy in copies:
        copy.start()
    for copy in copies:
        copy.wait()


def pick_kernel(place, where, x_ref, window_ref, own_ref):
    members, window = window_ref.shape[:2]
    groups = own_ref.shape[0]
    chip, core = where[0], where[1]
    for k in range(members):

        def tile(t):
            p = place[core * members + k, t]
            block = x_ref[jnp.maximum(p, 0), k]
            return jnp.where(p >= 0, block, jnp.zeros_like(block))

        for s in range(window):
            window_ref[k, s] = tile(chip * window + s)
        for g in range(groups):
            own_ref[g, k] = tile(g * window + chip)


def product_kernel(place, where, a_ref, *refs):
    inputs = NL * NX
    parts, outs = refs[:inputs], refs[inputs : inputs + NH * NY]
    panel, order, sems = refs[inputs + NH * NY :]
    members, window, _, _, size = panel.shape
    half = window // NC
    chip, core, group, x, l, h, y = (where[i] for i in range(7))
    step = pl.program_id(0)
    tile = group * window + lax.rem(h + step // NY, NH) * NY + lax.rem(y + step, NY)

    @pl.when(step == 0)
    def _():
        copies = []
        for side in range(NL):
            for hop, shift in enumerate(RING):
                source = lax.rem(x + shift, NX) * NL + lax.rem(l + side, NL)
                i = side * NX + hop
                copies.append(pltpu.make_async_copy(parts[i], panel.at[:, :, source], sems.at[i]))
        for copy in copies:
            copy.start()
        for k in range(members):
            listed = [place[core * members + k, chip * window + s] >= 0 for s in range(window)]
            count = sum(jnp.where(f, 1, 0) for f in listed)
            order[k, window] = count
            front, back = jnp.int32(0), count
            for s in range(window):
                order[k, jnp.where(listed[s], front, back)] = s
                front = front + jnp.where(listed[s], 1, 0)
                back = back + jnp.where(listed[s], 0, 1)
        for copy in copies:
            copy.wait()

    for k in range(members):
        cols = slice(k * size, (k + 1) * size)
        wanted = place[core * members + k, tile] >= 0
        few = order[k, window] <= half

        def store(values):
            for j, out in enumerate(outs):

                @pl.when(step == j)
                def _():
                    out[:, cols] = values

        def finish(tiles):
            values = jnp.zeros((size, size), F32)
            for s in tiles:
                start = pl.multiple_of(lax.rem(s, half) * size, size)
                left = a_ref[lax.div(s, half), :, pl.ds(start, size)]
                values += jnp.dot(left, panel[k, s].reshape(size, size), preferred_element_type=F32)
            level = level_of(jnp.max(jnp.abs(values), axis=0, keepdims=True))
            tail = jnp.broadcast_to(level, (16, size)).astype(jnp.int32).astype(I16)
            store(jnp.concatenate([code(values, level), tail], axis=0))

        @pl.when(jnp.logical_and(wanted, few))
        def _():
            finish([order[k, i] for i in range(half)])

        @pl.when(jnp.logical_and(wanted, jnp.logical_not(few)))
        def _():
            finish([jnp.int32(s) for s in range(window)])

        @pl.when(jnp.logical_not(wanted))
        def _():
            store(jnp.zeros((size + 16, size), I16))


def diagonal_kernel(place, where, *refs):
    count = NH * NY
    coded, parts, (d_ref, block) = refs[:count], refs[count : 2 * count], refs[2 * count :]
    _, members, _, size = parts[0].shape
    core, group, h, y = where[1], where[2], where[5], where[6]
    block[...] = jnp.zeros_like(block)
    for side in range(NH):
        for hop, shift in enumerate(RING):
            tile = lax.rem(h + side, NH) * NY + lax.rem(y + shift, NY)
            q_ref, ref = coded[side * NY + shift], parts[side * NY + hop]
            for k in range(members):
                cols = slice(k * size, (k + 1) * size)

                @pl.when(place[core * members + k, group * count + tile] >= 0)
                def _():
                    own = ref[:, k].reshape(size, size)
                    rest = plain(q_ref[:size, cols])
                    high = rest.astype(BF16)
                    low = (rest - high.astype(F32)).astype(BF16)
                    total = sum(
                        lax.dot_general(
                            own, term, (((0,), (0,)), ((), ())), preferred_element_type=F32
                        )
                        for term in (high, low)
                    )
                    block[:, cols] -= total * scale_of(plain(q_ref[size : size + 16, cols])[:1])

    values = block[...]
    level = level_of(jnp.max(jnp.abs(values), keepdims=True))
    width = values.shape[1] // 2
    for i in range(2):
        d_ref[i, :, :width] = code(values[:, i * width : (i + 1) * width], level)
        d_ref[i, :, width:] = jnp.broadcast_to(level, (size, LANES)).astype(jnp.int32).astype(I16)


def finish_kernel(place, where, *refs):
    parts, (u_ref, swap_ref) = refs[:-2], refs[-2:]
    sources = len(parts)
    slab, width = u_ref.shape
    size = 2 * slab
    members = width // size
    chip, core, group = where[0], where[1], where[2]
    mine = group * sources + chip
    for k in range(members):
        cols = slice(k * size, (k + 1) * size)
        total = jnp.zeros((size, size), F32)
        for ref in parts:
            scale = scale_of(plain(ref[size : size + 16, cols])[:1])
            total += plain(ref[:size, cols]) * scale
        keep = place[core * members + k, mine] >= 0
        rounded = jnp.where(keep, -total, jnp.zeros_like(total)).astype(BF16)
        first = core == 0
        u_ref[:, cols] = jnp.where(first, rounded[:slab], rounded[slab:])
        swap_ref[:, cols] = jnp.where(first, rounded[slab:], rounded[:slab])


def sum_of(q_ref):
    width = q_ref.shape[2] - LANES
    scale = scale_of(plain(q_ref[:, :, width:]))
    sums = [
        jnp.sum(plain(q_ref[:, :, i : i + LANES]) * scale, axis=0) for i in range(0, width, LANES)
    ]
    return jnp.concatenate(sums, axis=1)


def send(o_ref, values):
    level = level_of(jnp.max(jnp.abs(values), keepdims=True))
    tail = jnp.broadcast_to(level, (values.shape[0], LANES)).astype(jnp.int32).astype(I16)
    coded = jnp.concatenate([code(values, level), tail], axis=1)
    for j in range(o_ref.shape[0]):
        o_ref[j] = coded


def partial_kernel(q_ref, o_ref):
    send(o_ref, sum_of(q_ref))


def piece_kernel(q_ref, inverse_ref, o_ref):
    send(o_ref, inverse_ref[...] - sum_of(q_ref))


def total_kernel(q_ref, o_ref):
    pieces, cores, depth, reach = q_ref.shape
    supers, size, _ = o_ref.shape
    width = reach - LANES
    count = pieces // 2
    for c in range(cores):
        for g in range(pieces):
            rows = slice(g % count * depth, (g % count + 1) * depth)
            scale = scale_of(plain(q_ref[g, c, :, width:]))
            for t in range(width // LANES):
                column = g // count * width + t * LANES
                k = c * (supers // cores) + column // size
                lane = column % size
                o_ref[k, rows, lane : lane + LANES] = (
                    plain(q_ref[g, c, :, t * LANES : (t + 1) * LANES]) * scale
                )


def spread(own, axis, up):
    below = lax.ppermute(own, axis, UP)
    above = lax.ppermute(own, axis, DOWN)
    far = lax.ppermute(below, axis, UP) if up else lax.ppermute(above, axis, DOWN)
    return [own, below, above, far]


RING = (0, 3, 1, 2)


def update(ancestor_inv, lfactor, struct, validity, diag_inverse):
    rows, cols = ancestor_inv.shape
    entries, size, supers, _ = lfactor.shape
    groups = NX * NL
    chips = NH * NY
    part = size // groups
    members = supers // NC
    width = members * size
    group = lax.axis_index(XL)
    chip = lax.axis_index(HY)
    core = lax.axis_index("c")
    listed = struct.shape[1]
    tiles = rows * groups // size
    window = tiles // chips
    smem = pl.BlockSpec(memory_space=pltpu.SMEM)
    vmem = pl.BlockSpec(memory_space=pltpu.VMEM)

    other = lax.ppermute(ancestor_inv, "c", CORE_SWAP)

    hits = (struct[:, :, None] == jnp.arange(tiles, dtype=jnp.int32)) & (validity[:, :, None] > 0)
    position = jnp.arange(listed, dtype=jnp.int32)[None, :, None]
    place = jnp.max(jnp.where(hits, position, -1), axis=1)
    where = jnp.stack([chip, core, group] + [lax.axis_index(a) for a in ("x", "l", "h", "y")])

    share = pl.pallas_call(
        share_kernel,
        out_shape=jax.ShapeDtypeStruct((chips * NC, entries, members, part, size), BF16),
        in_specs=[smem, pl.BlockSpec(memory_space=pltpu.HBM)],
        out_specs=vmem,
        scratch_shapes=[
            pltpu.VMEM((entries, supers, part, size), BF16),
            pltpu.SemaphoreType.DMA,
        ],
        name="share",
    )(where, jnp.transpose(lfactor, (0, 2, 1, 3)))
    share = lax.all_to_all(share, ("h", "y", "c"), split_axis=0, concat_axis=0, tiled=True)
    share = share.reshape(listed, members, part, size)

    block = jax.ShapeDtypeStruct((members, window, part, size), BF16)
    near, own = pl.pallas_call(
        pick_kernel,
        out_shape=[block, jax.ShapeDtypeStruct((groups, members, part, size), BF16)],
        in_specs=[smem, smem, vmem],
        out_specs=[vmem] * 2,
        compiler_params=pltpu.CompilerParams(vmem_limit_bytes=8 << 20),
        name="pick",
    )(place, where, share)
    across = lax.ppermute(near, "l", CORE_SWAP)
    window_parts = spread(near, "x", True)
    window_parts += spread(across, "x", False)
    own = lax.all_to_all(own, XL, split_axis=0, concat_axis=0, tiled=True)
    across = lax.ppermute(own, "h", CORE_SWAP)
    row_parts = spread(own, "y", True)
    row_parts += spread(across, "y", False)

    staged = pl.pallas_call(
        stage_kernel,
        out_shape=jax.ShapeDtypeStruct((NC, rows, cols), BF16),
        in_specs=[smem, pl.BlockSpec(memory_space=pl.ANY), pl.BlockSpec(memory_space=pl.ANY)],
        out_specs=pl.BlockSpec(memory_space=pl.ANY),
        scratch_shapes=[pltpu.SemaphoreType.DMA((2,))],
        compiler_params=pltpu.CompilerParams(vmem_limit_bytes=1 << 20),
        name="stage",
    )(where, ancestor_inv, other)

    def row_tile(j, _, where):
        return 0, lax.rem(where[5] + j // NY, NH) * NY + lax.rem(where[6] + j, NY), 0

    coded = pl.pallas_call(
        product_kernel,
        out_shape=[jax.ShapeDtypeStruct((size + 16, width), I16)] * chips,
        grid_spec=pltpu.PrefetchScalarGridSpec(
            num_scalar_prefetch=2,
            grid=(chips,),
            in_specs=[pl.BlockSpec((NC, size, cols), row_tile)]
            + [pl.BlockSpec(memory_space=pltpu.HBM)] * len(window_parts),
            out_specs=[vmem] * chips,
            scratch_shapes=[
                pltpu.VMEM((members, window, groups, part, size), BF16),
                pltpu.SMEM((members, window + 1), jnp.int32),
                pltpu.SemaphoreType.DMA((len(window_parts),)),
            ],
        ),
        compiler_params=pltpu.CompilerParams(vmem_limit_bytes=20 << 20),
        name="product",
    )(place, where, staged, *window_parts)
    depth = 2 * size // groups
    reach = width // 2 + LANES
    diag = pl.pallas_call(
        diagonal_kernel,
        out_shape=jax.ShapeDtypeStruct((2, size, reach), I16),
        in_specs=[smem, smem] + [vmem] * (chips + len(row_parts)),
        out_specs=vmem,
        scratch_shapes=[pltpu.VMEM((size, width), F32)],
        compiler_params=pltpu.CompilerParams(vmem_limit_bytes=16 << 20),
        name="diagonal",
    )(place, where, *coded, *row_parts)

    sums = [coded[0]]
    for shifts in ((6, 5, 7), (2, 4, 1, 3)):
        for j in shifts:
            to = [
                (h * NY + y, (h + j // NY) % NH * NY + (y + j) % NY)
                for h in range(NH)
                for y in range(NY)
            ]
            sums.append(lax.ppermute(coded[j], HY, to))
    slab = jax.ShapeDtypeStruct((size // NC, width), BF16)
    mine, theirs = pl.pallas_call(
        finish_kernel,
        out_shape=[slab, slab],
        in_specs=[smem, smem] + [vmem] * len(sums),
        out_specs=[vmem] * 2,
        compiler_params=pltpu.CompilerParams(vmem_limit_bytes=12 << 20),
        name="finish",
    )(place, where, *sums)

    theirs = lax.ppermute(theirs, "c", CORE_SWAP)
    column_block = jnp.where(
        core == 0,
        jnp.concatenate([mine, theirs], axis=1),
        jnp.concatenate([theirs, mine], axis=1),
    )

    small = pltpu.CompilerParams(vmem_limit_bytes=6 << 20)
    diag = diag.reshape(groups, depth, reach)
    diag = lax.all_to_all(diag, XL, split_axis=0, concat_axis=0, tiled=True)
    diag = pl.pallas_call(
        partial_kernel,
        out_shape=jax.ShapeDtypeStruct((chips, depth, reach), I16),
        in_specs=[vmem],
        out_specs=vmem,
        compiler_params=small,
        name="partial",
    )(diag)
    diag = lax.all_to_all(diag, HY, split_axis=0, concat_axis=0, tiled=True)
    inverse = lax.dynamic_slice(
        diag_inverse,
        (core * members, group % (groups // 2) * depth, 0),
        (members, depth, size),
    )
    inverse = jnp.transpose(inverse, (1, 0, 2)).reshape(depth, 2, width // 2)
    inverse = lax.dynamic_index_in_dim(inverse, group // (groups // 2), 1, keepdims=False)
    piece = pl.pallas_call(
        piece_kernel,
        out_shape=jax.ShapeDtypeStruct((groups * NC, depth, reach), I16),
        in_specs=[vmem, vmem],
        out_specs=vmem,
        compiler_params=pltpu.CompilerParams(vmem_limit_bytes=60 << 20),
        name="piece",
    )(diag, inverse)
    whole = lax.all_to_all(piece, XL + ("c",), split_axis=0, concat_axis=0, tiled=True)
    diagonal = pl.pallas_call(
        total_kernel,
        out_shape=jax.ShapeDtypeStruct(diag_inverse.shape, F32),
        in_specs=[vmem],
        out_specs=vmem,
        compiler_params=pltpu.CompilerParams(vmem_limit_bytes=12 << 20),
        name="total",
    )(whole.reshape(groups, NC, depth, reach))
    return column_block, diagonal


def solution(mesh):
    fine = Mesh(mesh.devices.reshape(NX, NL, NH, NY, NC), ("x", "l", "h", "y", "c"))
    return jax.shard_map(
        update,
        mesh=fine,
        in_specs=(P(XL, ("h", "y", "c")), P(("h", "y", "c")), P(), P(), P()),
        out_specs=(P(("x", "l", "h", "y", "c")), P()),
        check_vma=False,
    )
```

```python
import functools

import jax
import jax.numpy as jnp
from jax import lax
from jax.experimental import pallas as pl
from jax.experimental.pallas import tpu as pltpu
from jax.sharding import Mesh, PartitionSpec as P


BF16 = jnp.bfloat16
F32 = jnp.float32
I16 = jnp.int16
NX, NL, NH, NY, NC = 4, 2, 2, 4, 2
XL = ("x", "l")
HY = ("h", "y")
CHIPS = XL + HY
CORE_SWAP = [(0, 1), (1, 0)]
UP = [(i, (i + 1) % NX) for i in range(NX)]
DOWN = [(i, (i - 1) % NX) for i in range(NX)]
LEVELS = 32000.0
LOWEST = -100.0
LANES = 128


def level_of(top):
    return jnp.maximum(jnp.ceil(jnp.log2(jnp.maximum(top, 1e-37)) + 0.01), LOWEST)


def code(values, level):
    return jnp.round(values * (jnp.exp2(-level) * LEVELS)).astype(jnp.int32).astype(I16)


def plain(coded):
    return coded.astype(jnp.int32).astype(F32)


def scale_of(level):
    return jnp.exp2(level) * (1.0 / LEVELS)


def share_kernel(where, l_ref, o_ref, buffer, sem):
    part = o_ref.shape[3]
    copy = pltpu.make_async_copy(
        l_ref.at[:, :, pl.ds(pl.multiple_of(where[2] * part, part), part)], buffer, sem
    )
    copy.start()
    copy.wait()
    members = o_ref.shape[2]
    for i in range(o_ref.shape[0]):
        core = i % NC
        o_ref[i] = buffer[:, core * members : (core + 1) * members]


def stage_kernel(where, own_ref, other_ref, near_ref, below_ref, o_ref, parts_ref, sems):
    core = where[1]
    copies = [
        pltpu.make_async_copy(own_ref, o_ref.at[core], sems.at[0]),
        pltpu.make_async_copy(other_ref, o_ref.at[1 - core], sems.at[1]),
        pltpu.make_async_copy(near_ref, parts_ref.at[0], sems.at[2]),
        pltpu.make_async_copy(below_ref, parts_ref.at[1], sems.at[3]),
    ]
    for copy in copies:
        copy.start()
    for copy in copies:
        copy.wait()


def pick_kernel(place, where, x_ref, window_ref, own_ref):
    members, window = window_ref.shape[:2]
    groups = own_ref.shape[0]
    chip, core = where[0], where[1]
    for k in range(members):

        def tile(t):
            p = place[core * members + k, t]
            block = x_ref[jnp.maximum(p, 0), k]
            return jnp.where(p >= 0, block, jnp.zeros_like(block))

        for s in range(window):
            window_ref[k, s] = tile(chip * window + s)
        for g in range(groups):
            own_ref[g, k] = tile(g * window + chip)


def list_window(place, where, order):
    members, window = order.shape[0], order.shape[1] - 1
    chip, core = where[0], where[1]
    for k in range(members):
        listed = [place[core * members + k, chip * window + s] >= 0 for s in range(window)]
        count = sum(jnp.where(f, 1, 0) for f in listed)
        order[k, window] = count
        front, back = jnp.int32(0), count
        for s in range(window):
            order[k, jnp.where(listed[s], front, back)] = s
            front = front + jnp.where(listed[s], 1, 0)
            back = back + jnp.where(listed[s], 0, 1)


def first_kernel(shifts, place, where, a_ref, first_parts, *refs):
    inputs = NL * NX - 2
    parts, outs = refs[:inputs], refs[inputs : inputs + len(shifts)]
    panel, order, sems = refs[inputs + len(shifts) :]
    x, l = where[3], where[4]

    @pl.when(pl.program_id(0) == 0)
    def _():
        copies = []
        for side in range(NL):
            for hop, shift in enumerate(RING):
                source = lax.rem(x + shift, NX) * NL + lax.rem(l + side, NL)
                i = side * NX + hop
                part = first_parts.at[i] if i < 2 else parts[i - 2]
                copies.append(pltpu.make_async_copy(part, panel.at[:, :, source], sems.at[i]))
        for copy in copies:
            copy.start()
        list_window(place, where, order)
        for copy in copies:
            copy.wait()

    products(shifts, place, where, a_ref, panel, order, outs)


def second_kernel(shifts, place, where, a_ref, panel, *refs):
    outs, order = refs[:-1], refs[-1]

    @pl.when(pl.program_id(0) == 0)
    def _():
        list_window(place, where, order)

    products(shifts, place, where, a_ref, panel, order, outs)


def products(shifts, place, where, a_ref, panel, order, outs):
    members, window, _, _, size = panel.shape
    half = window // NC
    core, group, h, y = where[1], where[2], where[5], where[6]
    step = pl.program_id(0)
    j = step + shifts[0]
    tile = group * window + lax.rem(h + lax.div(j, NY), NH) * NY + lax.rem(y + j, NY)

    for k in range(members):
        cols = slice(k * size, (k + 1) * size)
        wanted = place[core * members + k, tile] >= 0
        few = order[k, window] <= half

        def store(values):
            for i, out in enumerate(outs):

                @pl.when(step == i)
                def _():
                    out[:, cols] = values

        def finish(tiles):
            values = jnp.zeros((size, size), F32)
            for s in tiles:
                start = pl.multiple_of(lax.rem(s, half) * size, size)
                left = a_ref[lax.div(s, half), :, pl.ds(start, size)]
                values += jnp.dot(left, panel[k, s].reshape(size, size), preferred_element_type=F32)
            level = level_of(jnp.max(jnp.abs(values), axis=0, keepdims=True))
            tail = jnp.broadcast_to(level, (16, size)).astype(jnp.int32).astype(I16)
            store(jnp.concatenate([code(values, level), tail], axis=0))

        @pl.when(jnp.logical_and(wanted, few))
        def _():
            finish([order[k, i] for i in range(half)])

        @pl.when(jnp.logical_and(wanted, jnp.logical_not(few)))
        def _():
            finish([jnp.int32(s) for s in range(window)])

        @pl.when(jnp.logical_not(wanted))
        def _():
            store(jnp.zeros((size + 16, size), I16))


def diagonal_kernel(place, where, *refs):
    count = NH * NY
    coded, parts, (d_ref, block) = refs[:count], refs[count : 2 * count], refs[2 * count :]
    _, members, _, size = parts[0].shape
    core, group, h, y = where[1], where[2], where[5], where[6]
    block[...] = jnp.zeros_like(block)
    for side in range(NH):
        for hop, shift in enumerate(RING):
            tile = lax.rem(h + side, NH) * NY + lax.rem(y + shift, NY)
            q_ref, ref = coded[side * NY + shift], parts[side * NY + hop]
            for k in range(members):
                cols = slice(k * size, (k + 1) * size)

                @pl.when(place[core * members + k, group * count + tile] >= 0)
                def _():
                    own = ref[:, k].reshape(size, size)
                    rest = plain(q_ref[:size, cols])
                    high = rest.astype(BF16)
                    low = (rest - high.astype(F32)).astype(BF16)
                    total = sum(
                        lax.dot_general(
                            own, term, (((0,), (0,)), ((), ())), preferred_element_type=F32
                        )
                        for term in (high, low)
                    )
                    block[:, cols] -= total * scale_of(plain(q_ref[size : size + 16, cols])[:1])

    values = block[...]
    level = level_of(jnp.max(jnp.abs(values), keepdims=True))
    width = values.shape[1] // 2
    for i in range(2):
        d_ref[i, :, :width] = code(values[:, i * width : (i + 1) * width], level)
        d_ref[i, :, width:] = jnp.broadcast_to(level, (size, LANES)).astype(jnp.int32).astype(I16)


def finish_kernel(place, where, *refs):
    parts, (u_ref, swap_ref) = refs[:-2], refs[-2:]
    sources = len(parts)
    slab, width = u_ref.shape
    size = 2 * slab
    members = width // size
    chip, core, group = where[0], where[1], where[2]
    mine = group * sources + chip
    for k in range(members):
        cols = slice(k * size, (k + 1) * size)
        total = jnp.zeros((size, size), F32)
        for ref in parts:
            scale = scale_of(plain(ref[size : size + 16, cols])[:1])
            total += plain(ref[:size, cols]) * scale
        keep = place[core * members + k, mine] >= 0
        rounded = jnp.where(keep, -total, jnp.zeros_like(total)).astype(BF16)
        first = core == 0
        u_ref[:, cols] = jnp.where(first, rounded[:slab], rounded[slab:])
        swap_ref[:, cols] = jnp.where(first, rounded[slab:], rounded[:slab])


def piece_kernel(q_ref, inverse_ref, o_ref):
    width = q_ref.shape[2] - LANES
    scale = scale_of(plain(q_ref[:, :, width:]))
    sums = [
        jnp.sum(plain(q_ref[:, :, i : i + LANES]) * scale, axis=0) for i in range(0, width, LANES)
    ]
    values = inverse_ref[...] - jnp.concatenate(sums, axis=1)
    level = level_of(jnp.max(jnp.abs(values), keepdims=True))
    coded = jnp.concatenate(
        [
            code(values, level),
            jnp.broadcast_to(level, (values.shape[0], LANES)).astype(jnp.int32).astype(I16),
        ],
        axis=1,
    )
    for j in range(o_ref.shape[0]):
        o_ref[j] = coded


def total_kernel(q_ref, o_ref):
    pieces, cores, depth, reach = q_ref.shape
    supers, size, _ = o_ref.shape
    width = reach - LANES
    count = pieces // 2
    for c in range(cores):
        for i in range(2):
            rows = slice(i * count, (i + 1) * count)
            scale = scale_of(plain(q_ref[rows, c, :, width:]))
            for t in range(width // LANES):
                lane = (i * width + t * LANES) % size
                k = c * (supers // cores) + (i * width + t * LANES) // size
                values = plain(q_ref[rows, c, :, t * LANES : (t + 1) * LANES]) * scale
                o_ref[k, :, lane : lane + LANES] = values.reshape(count * depth, LANES)


def spread(own, axis, up):
    below = lax.ppermute(own, axis, UP)
    above = lax.ppermute(own, axis, DOWN)
    far = lax.ppermute(below, axis, UP) if up else lax.ppermute(above, axis, DOWN)
    return [own, below, above, far]


RING = (0, 3, 1, 2)


def update(ancestor_inv, lfactor, struct, validity, diag_inverse):
    rows, cols = ancestor_inv.shape
    entries, size, supers, _ = lfactor.shape
    groups = NX * NL
    chips = NH * NY
    part = size // groups
    members = supers // NC
    width = members * size
    group = lax.axis_index(XL)
    chip = lax.axis_index(HY)
    core = lax.axis_index("c")
    listed = struct.shape[1]
    tiles = rows * groups // size
    window = tiles // chips
    smem = pl.BlockSpec(memory_space=pltpu.SMEM)
    vmem = pl.BlockSpec(memory_space=pltpu.VMEM)

    other = lax.ppermute(ancestor_inv, "c", CORE_SWAP)

    hits = (struct[:, :, None] == jnp.arange(tiles, dtype=jnp.int32)) & (validity[:, :, None] > 0)
    position = jnp.arange(listed, dtype=jnp.int32)[None, :, None]
    place = jnp.max(jnp.where(hits, position, -1), axis=1)
    where = jnp.stack([chip, core, group] + [lax.axis_index(a) for a in ("x", "l", "h", "y")])

    share = pl.pallas_call(
        share_kernel,
        out_shape=jax.ShapeDtypeStruct((chips * NC, entries, members, part, size), BF16),
        in_specs=[smem, pl.BlockSpec(memory_space=pltpu.HBM)],
        out_specs=vmem,
        scratch_shapes=[
            pltpu.VMEM((entries, supers, part, size), BF16),
            pltpu.SemaphoreType.DMA,
        ],
        name="share",
    )(where, jnp.transpose(lfactor, (0, 2, 1, 3)))
    share = lax.all_to_all(share, ("h", "y", "c"), split_axis=0, concat_axis=0, tiled=True)
    share = share.reshape(listed, members, part, size)

    block = jax.ShapeDtypeStruct((members, window, part, size), BF16)
    near, own = pl.pallas_call(
        pick_kernel,
        out_shape=[block, jax.ShapeDtypeStruct((groups, members, part, size), BF16)],
        in_specs=[smem, smem, vmem],
        out_specs=[vmem] * 2,
        compiler_params=pltpu.CompilerParams(vmem_limit_bytes=8 << 20),
        name="pick",
    )(place, where, share)
    across = lax.ppermute(near, "l", CORE_SWAP)
    window_parts = spread(near, "x", True)
    window_parts += spread(across, "x", False)
    own = lax.all_to_all(own, XL, split_axis=0, concat_axis=0, tiled=True)
    across = lax.ppermute(own, "h", CORE_SWAP)
    row_parts = spread(own, "y", True)
    row_parts += spread(across, "y", False)

    anywhere = pl.BlockSpec(memory_space=pl.ANY)
    staged, first_parts = pl.pallas_call(
        stage_kernel,
        out_shape=[
            jax.ShapeDtypeStruct((NC, rows, cols), BF16),
            jax.ShapeDtypeStruct((2, members, window, part, size), BF16),
        ],
        in_specs=[smem] + [anywhere] * 4,
        out_specs=[anywhere] * 2,
        scratch_shapes=[pltpu.SemaphoreType.DMA((4,))],
        compiler_params=pltpu.CompilerParams(vmem_limit_bytes=1 << 20),
        name="stage",
    )(where, ancestor_inv, other, *window_parts[:2])

    def row_tile(shifts):
        def index(i, _, where):
            j = i + shifts[0]
            tile = lax.rem(where[5] + lax.div(j, NY), NH) * NY + lax.rem(where[6] + j, NY)
            return 0, tile, 0

        return pl.BlockSpec((NC, size, cols), index)

    panel = jax.ShapeDtypeStruct((members, window, groups, part, size), BF16)
    block = jax.ShapeDtypeStruct((size + 16, width), I16)
    order = pltpu.SMEM((members, window + 1), jnp.int32)
    params = pltpu.CompilerParams(vmem_limit_bytes=20 << 20)
    late, early = tuple(range(5)), tuple(range(5, chips))
    *coded_early, panel = pl.pallas_call(
        functools.partial(first_kernel, early),
        out_shape=[block] * len(early) + [panel],
        grid_spec=pltpu.PrefetchScalarGridSpec(
            num_scalar_prefetch=2,
            grid=(len(early),),
            in_specs=[row_tile(early)] + [anywhere] * (len(window_parts) - 1),
            out_specs=[vmem] * (len(early) + 1),
            scratch_shapes=[order, pltpu.SemaphoreType.DMA((len(window_parts),))],
        ),
        compiler_params=params,
        name="first",
    )(place, where, staged, first_parts, *window_parts[2:])
    coded = pl.pallas_call(
        functools.partial(second_kernel, late),
        out_shape=[block] * len(late),
        grid_spec=pltpu.PrefetchScalarGridSpec(
            num_scalar_prefetch=2,
            grid=(len(late),),
            in_specs=[row_tile(late), vmem],
            out_specs=[vmem] * len(late),
            scratch_shapes=[order],
        ),
        compiler_params=params,
        name="second",
    )(place, where, staged, panel)
    coded = list(coded) + list(coded_early)

    pieces = groups * chips

    depth = 2 * size // pieces
    reach = width // 2 + LANES
    diag = pl.pallas_call(
        diagonal_kernel,
        out_shape=jax.ShapeDtypeStruct((2, size, reach), I16),
        in_specs=[smem, smem] + [vmem] * (chips + len(row_parts)),
        out_specs=vmem,
        scratch_shapes=[pltpu.VMEM((size, width), F32)],
        compiler_params=pltpu.CompilerParams(vmem_limit_bytes=16 << 20),
        name="diagonal",
    )(place, where, *coded, *row_parts)

    sums = [coded[0]]
    for shifts in ((6, 5, 7), (4, 2), (1, 3)):
        for j in shifts:
            to = [
                (h * NY + y, (h + j // NY) % NH * NY + (y + j) % NY)
                for h in range(NH)
                for y in range(NY)
            ]
            sums.append(lax.ppermute(coded[j], HY, to))
    slab = jax.ShapeDtypeStruct((size // NC, width), BF16)
    mine, theirs = pl.pallas_call(
        finish_kernel,
        out_shape=[slab, slab],
        in_specs=[smem, smem] + [vmem] * len(sums),
        out_specs=[vmem] * 2,
        compiler_params=pltpu.CompilerParams(vmem_limit_bytes=12 << 20),
        name="finish",
    )(place, where, *sums)

    theirs = lax.ppermute(theirs, "c", CORE_SWAP)
    column_block = jnp.where(
        core == 0,
        jnp.concatenate([mine, theirs], axis=1),
        jnp.concatenate([theirs, mine], axis=1),
    )

    diag = diag.reshape(pieces, depth, reach)
    diag = lax.all_to_all(diag, CHIPS, split_axis=0, concat_axis=0, tiled=True)
    index = group * chips + chip
    inverse = lax.dynamic_slice(
        diag_inverse,
        (core * members, index % (pieces // 2) * depth, 0),
        (members, depth, size),
    )
    inverse = jnp.transpose(inverse, (1, 0, 2)).reshape(depth, 2, width // 2)
    inverse = lax.dynamic_index_in_dim(inverse, index // (pieces // 2), 1, keepdims=False)
    piece = pl.pallas_call(
        piece_kernel,
        out_shape=jax.ShapeDtypeStruct((pieces * NC, depth, reach), I16),
        in_specs=[vmem, vmem],
        out_specs=vmem,
        compiler_params=pltpu.CompilerParams(vmem_limit_bytes=6 << 20),
        name="piece",
    )(diag, inverse)
    whole = lax.all_to_all(piece, CHIPS + ("c",), split_axis=0, concat_axis=0, tiled=True)
    diagonal = pl.pallas_call(
        total_kernel,
        out_shape=jax.ShapeDtypeStruct(diag_inverse.shape, F32),
        in_specs=[vmem],
        out_specs=vmem,
        compiler_params=pltpu.CompilerParams(vmem_limit_bytes=12 << 20),
        name="total",
    )(whole.reshape(pieces, NC, depth, reach))
    return column_block, diagonal


def solution(mesh):
    fine = Mesh(mesh.devices.reshape(NX, NL, NH, NY, NC), ("x", "l", "h", "y", "c"))
    return jax.shard_map(
        update,
        mesh=fine,
        in_specs=(P(XL, ("h", "y", "c")), P(("h", "y", "c")), P(), P(), P()),
        out_specs=(P(("x", "l", "h", "y", "c")), P()),
        check_vma=False,
    )
```

```python
import functools

import jax
import jax.numpy as jnp
from jax import lax
from jax.experimental import pallas as pl
from jax.experimental.pallas import tpu as pltpu
from jax.sharding import Mesh, PartitionSpec as P


BF16 = jnp.bfloat16
F32 = jnp.float32
I16 = jnp.int16
NX, NL, NH, NY, NC = 4, 2, 2, 4, 2
XL = ("x", "l")
HY = ("h", "y")
CHIPS = XL + HY
CORE_SWAP = [(0, 1), (1, 0)]
UP = [(i, (i + 1) % NX) for i in range(NX)]
DOWN = [(i, (i - 1) % NX) for i in range(NX)]
LEVELS = 32000.0
LOWEST = -100.0
LANES = 128
TAIL = 8


def level_of(top):
    return jnp.maximum(jnp.ceil(jnp.log2(jnp.maximum(top, 1e-37)) + 0.01), LOWEST)


def code(values, level):
    return jnp.round(values * (jnp.exp2(-level) * LEVELS)).astype(jnp.int32).astype(I16)


def plain(coded):
    return coded.astype(jnp.int32).astype(F32)


def scale_of(level):
    return jnp.exp2(level) * (1.0 / LEVELS)


def share_kernel(where, l_ref, o_ref, buffer, sem):
    part = o_ref.shape[3]
    copy = pltpu.make_async_copy(
        l_ref.at[:, :, pl.ds(pl.multiple_of(where[2] * part, part), part)], buffer, sem
    )
    copy.start()
    copy.wait()
    members = o_ref.shape[2]
    for i in range(o_ref.shape[0]):
        core = i % NC
        o_ref[i] = buffer[:, core * members : (core + 1) * members]


def stage_kernel(where, own_ref, other_ref, near_ref, below_ref, o_ref, parts_ref, sems):
    core = where[1]
    copies = [
        pltpu.make_async_copy(own_ref, o_ref.at[core], sems.at[0]),
        pltpu.make_async_copy(other_ref, o_ref.at[1 - core], sems.at[1]),
        pltpu.make_async_copy(near_ref, parts_ref.at[0], sems.at[2]),
        pltpu.make_async_copy(below_ref, parts_ref.at[1], sems.at[3]),
    ]
    for copy in copies:
        copy.start()
    for copy in copies:
        copy.wait()


def pick_kernel(place, where, x_ref, window_ref, own_ref):
    members, window = window_ref.shape[:2]
    groups = own_ref.shape[0]
    chip, core = where[0], where[1]
    for k in range(members):

        def tile(t):
            p = place[core * members + k, t]
            block = x_ref[jnp.maximum(p, 0), k]
            return jnp.where(p >= 0, block, jnp.zeros_like(block))

        for s in range(window):
            window_ref[k, s] = tile(chip * window + s)
        for g in range(groups):
            own_ref[g, k] = tile(g * window + chip)


def list_window(place, where, order):
    members, window = order.shape[0], order.shape[1] - 1
    chip, core = where[0], where[1]
    for k in range(members):
        listed = [place[core * members + k, chip * window + s] >= 0 for s in range(window)]
        count = sum(jnp.where(f, 1, 0) for f in listed)
        order[k, window] = count
        front, back = jnp.int32(0), count
        for s in range(window):
            order[k, jnp.where(listed[s], front, back)] = s
            front = front + jnp.where(listed[s], 1, 0)
            back = back + jnp.where(listed[s], 0, 1)


def first_kernel(shifts, place, where, a_ref, first_parts, *refs):
    inputs = NL * NX - 2
    parts, outs = refs[:inputs], refs[inputs : inputs + len(shifts)]
    panel, order, sems = refs[inputs + len(shifts) :]
    x, l = where[3], where[4]

    @pl.when(pl.program_id(0) == 0)
    def _():
        copies = []
        for side in range(NL):
            for hop, shift in enumerate(RING):
                source = lax.rem(x + shift, NX) * NL + lax.rem(l + side, NL)
                i = side * NX + hop
                part = first_parts.at[i] if i < 2 else parts[i - 2]
                copies.append(pltpu.make_async_copy(part, panel.at[:, :, source], sems.at[i]))
        for copy in copies:
            copy.start()
        list_window(place, where, order)
        for copy in copies:
            copy.wait()

    products(shifts, place, where, a_ref, panel, order, outs)


def second_kernel(shifts, place, where, a_ref, panel, *refs):
    outs, order = refs[:-1], refs[-1]

    @pl.when(pl.program_id(0) == 0)
    def _():
        list_window(place, where, order)

    products(shifts, place, where, a_ref, panel, order, outs)


def products(shifts, place, where, a_ref, panel, order, outs):
    members, window, _, _, size = panel.shape
    half = window // NC
    core, group, h, y = where[1], where[2], where[5], where[6]
    step = pl.program_id(0)
    j = step + shifts[0]
    tile = group * window + lax.rem(h + lax.div(j, NY), NH) * NY + lax.rem(y + j, NY)

    for k in range(members):
        cols = slice(k * size, (k + 1) * size)
        wanted = place[core * members + k, tile] >= 0
        few = order[k, window] <= half

        def store(values):
            for i, out in enumerate(outs):

                @pl.when(step == i)
                def _():
                    out[:, cols] = values

        def finish(tiles):
            values = jnp.zeros((size, size), F32)
            for s in tiles:
                start = pl.multiple_of(lax.rem(s, half) * size, size)
                left = a_ref[lax.div(s, half), :, pl.ds(start, size)]
                values += jnp.dot(left, panel[k, s].reshape(size, size), preferred_element_type=F32)
            level = level_of(jnp.max(jnp.abs(values), axis=0, keepdims=True))
            tail = jnp.broadcast_to(level, (TAIL, size)).astype(jnp.int32).astype(I16)
            store(jnp.concatenate([code(values, level), tail], axis=0))

        @pl.when(jnp.logical_and(wanted, few))
        def _():
            finish([order[k, i] for i in range(half)])

        @pl.when(jnp.logical_and(wanted, jnp.logical_not(few)))
        def _():
            finish([jnp.int32(s) for s in range(window)])

        @pl.when(jnp.logical_not(wanted))
        def _():
            store(jnp.zeros((size + TAIL, size), I16))


def diagonal_kernel(place, where, *refs):
    count = NH * NY
    coded, parts, (d_ref, block) = refs[:count], refs[count : 2 * count], refs[2 * count :]
    _, members, _, size = parts[0].shape
    core, group, h, y = where[1], where[2], where[5], where[6]
    block[...] = jnp.zeros_like(block)
    for side in range(NH):
        for hop, shift in enumerate(RING):
            tile = lax.rem(h + side, NH) * NY + lax.rem(y + shift, NY)
            q_ref, ref = coded[side * NY + shift], parts[side * NY + hop]
            for k in range(members):
                cols = slice(k * size, (k + 1) * size)

                @pl.when(place[core * members + k, group * count + tile] >= 0)
                def _():
                    own = jnp.transpose(ref[:, k].reshape(size, size))
                    rest = plain(q_ref[:size, cols])
                    high = rest.astype(BF16)
                    low = (rest - high.astype(F32)).astype(BF16)
                    both = jnp.dot(
                        own, jnp.concatenate([high, low], axis=1), preferred_element_type=F32
                    )
                    total = both[:, :size] + both[:, size:]
                    block[:, cols] -= total * scale_of(plain(q_ref[size : size + TAIL, cols])[:1])

    values = block[...]
    level = level_of(jnp.max(jnp.abs(values), keepdims=True))
    width = values.shape[1] // 2
    for i in range(2):
        d_ref[i, :, :width] = code(values[:, i * width : (i + 1) * width], level)
        d_ref[i, :, width:] = jnp.broadcast_to(level, (size, LANES)).astype(jnp.int32).astype(I16)


def finish_kernel(place, where, *refs):
    parts, (u_ref, swap_ref) = refs[:-2], refs[-2:]
    sources = len(parts)
    slab, width = u_ref.shape
    size = 2 * slab
    members = width // size
    chip, core, group = where[0], where[1], where[2]
    mine = group * sources + chip
    for k in range(members):
        cols = slice(k * size, (k + 1) * size)
        total = jnp.zeros((size, size), F32)
        for ref in parts:
            scale = scale_of(plain(ref[size : size + TAIL, cols])[:1])
            total += plain(ref[:size, cols]) * scale
        keep = place[core * members + k, mine] >= 0
        rounded = jnp.where(keep, -total, jnp.zeros_like(total)).astype(BF16)
        first = core == 0
        u_ref[:, cols] = jnp.where(first, rounded[:slab], rounded[slab:])
        swap_ref[:, cols] = jnp.where(first, rounded[slab:], rounded[:slab])


def piece_kernel(q_ref, inverse_ref, o_ref):
    width = q_ref.shape[2] - LANES
    scale = scale_of(plain(q_ref[:, :, width:]))
    sums = [
        jnp.sum(plain(q_ref[:, :, i : i + LANES]) * scale, axis=0) for i in range(0, width, LANES)
    ]
    values = inverse_ref[...] - jnp.concatenate(sums, axis=1)
    level = level_of(jnp.max(jnp.abs(values), keepdims=True))
    coded = jnp.concatenate(
        [
            code(values, level),
            jnp.broadcast_to(level, (values.shape[0], LANES)).astype(jnp.int32).astype(I16),
        ],
        axis=1,
    )
    for j in range(o_ref.shape[0]):
        o_ref[j] = coded


def total_kernel(q_ref, o_ref):
    pieces, cores, depth, reach = q_ref.shape
    supers, size, _ = o_ref.shape
    width = reach - LANES
    count = pieces // 2
    for c in range(cores):
        for i in range(2):
            rows = slice(i * count, (i + 1) * count)
            scale = scale_of(plain(q_ref[rows, c, :, width:]))
            for t in range(width // LANES):
                lane = (i * width + t * LANES) % size
                k = c * (supers // cores) + (i * width + t * LANES) // size
                values = plain(q_ref[rows, c, :, t * LANES : (t + 1) * LANES]) * scale
                o_ref[k, :, lane : lane + LANES] = values.reshape(count * depth, LANES)


def spread(own, axis, up):
    below = lax.ppermute(own, axis, UP)
    above = lax.ppermute(own, axis, DOWN)
    far = lax.ppermute(below, axis, UP) if up else lax.ppermute(above, axis, DOWN)
    return [own, below, above, far]


RING = (0, 3, 1, 2)


def update(ancestor_inv, lfactor, struct, validity, diag_inverse):
    rows, cols = ancestor_inv.shape
    entries, size, supers, _ = lfactor.shape
    groups = NX * NL
    chips = NH * NY
    part = size // groups
    members = supers // NC
    width = members * size
    group = lax.axis_index(XL)
    chip = lax.axis_index(HY)
    core = lax.axis_index("c")
    listed = struct.shape[1]
    tiles = rows * groups // size
    window = tiles // chips
    smem = pl.BlockSpec(memory_space=pltpu.SMEM)
    vmem = pl.BlockSpec(memory_space=pltpu.VMEM)

    other = lax.ppermute(ancestor_inv, "c", CORE_SWAP)

    hits = (struct[:, :, None] == jnp.arange(tiles, dtype=jnp.int32)) & (validity[:, :, None] > 0)
    position = jnp.arange(listed, dtype=jnp.int32)[None, :, None]
    place = jnp.max(jnp.where(hits, position, -1), axis=1)
    where = jnp.stack([chip, core, group] + [lax.axis_index(a) for a in ("x", "l", "h", "y")])

    share = pl.pallas_call(
        share_kernel,
        out_shape=jax.ShapeDtypeStruct((chips * NC, entries, members, part, size), BF16),
        in_specs=[smem, pl.BlockSpec(memory_space=pltpu.HBM)],
        out_specs=vmem,
        scratch_shapes=[
            pltpu.VMEM((entries, supers, part, size), BF16),
            pltpu.SemaphoreType.DMA,
        ],
        name="share",
    )(where, jnp.transpose(lfactor, (0, 2, 1, 3)))
    share = lax.all_to_all(share, ("h", "y", "c"), split_axis=0, concat_axis=0, tiled=True)
    share = share.reshape(listed, members, part, size)

    block = jax.ShapeDtypeStruct((members, window, part, size), BF16)
    near, own = pl.pallas_call(
        pick_kernel,
        out_shape=[block, jax.ShapeDtypeStruct((groups, members, part, size), BF16)],
        in_specs=[smem, smem, vmem],
        out_specs=[vmem] * 2,
        compiler_params=pltpu.CompilerParams(vmem_limit_bytes=8 << 20),
        name="pick",
    )(place, where, share)
    across = lax.ppermute(near, "l", CORE_SWAP)
    window_parts = spread(near, "x", True)
    window_parts += spread(across, "x", False)
    own = lax.all_to_all(own, XL, split_axis=0, concat_axis=0, tiled=True)
    across = lax.ppermute(own, "h", CORE_SWAP)
    row_parts = spread(own, "y", True)
    row_parts += spread(across, "y", False)

    anywhere = pl.BlockSpec(memory_space=pl.ANY)
    staged, first_parts = pl.pallas_call(
        stage_kernel,
        out_shape=[
            jax.ShapeDtypeStruct((NC, rows, cols), BF16),
            jax.ShapeDtypeStruct((2, members, window, part, size), BF16),
        ],
        in_specs=[smem] + [anywhere] * 4,
        out_specs=[anywhere] * 2,
        scratch_shapes=[pltpu.SemaphoreType.DMA((4,))],
        compiler_params=pltpu.CompilerParams(vmem_limit_bytes=1 << 20),
        name="stage",
    )(where, ancestor_inv, other, *window_parts[:2])

    def row_tile(shifts):
        def index(i, _, where):
            j = i + shifts[0]
            tile = lax.rem(where[5] + lax.div(j, NY), NH) * NY + lax.rem(where[6] + j, NY)
            return 0, tile, 0

        return pl.BlockSpec((NC, size, cols), index)

    panel = jax.ShapeDtypeStruct((members, window, groups, part, size), BF16)
    block = jax.ShapeDtypeStruct((size + TAIL, width), I16)
    order = pltpu.SMEM((members, window + 1), jnp.int32)
    params = pltpu.CompilerParams(vmem_limit_bytes=20 << 20)
    late, early = tuple(range(5)), tuple(range(5, chips))
    *coded_early, panel = pl.pallas_call(
        functools.partial(first_kernel, early),
        out_shape=[block] * len(early) + [panel],
        grid_spec=pltpu.PrefetchScalarGridSpec(
            num_scalar_prefetch=2,
            grid=(len(early),),
            in_specs=[row_tile(early)] + [anywhere] * (len(window_parts) - 1),
            out_specs=[vmem] * (len(early) + 1),
            scratch_shapes=[order, pltpu.SemaphoreType.DMA((len(window_parts),))],
        ),
        compiler_params=params,
        name="first",
    )(place, where, staged, first_parts, *window_parts[2:])
    coded = pl.pallas_call(
        functools.partial(second_kernel, late),
        out_shape=[block] * len(late),
        grid_spec=pltpu.PrefetchScalarGridSpec(
            num_scalar_prefetch=2,
            grid=(len(late),),
            in_specs=[row_tile(late), vmem],
            out_specs=[vmem] * len(late),
            scratch_shapes=[order],
        ),
        compiler_params=params,
        name="second",
    )(place, where, staged, panel)
    coded = list(coded) + list(coded_early)

    pieces = groups * chips

    depth = 2 * size // pieces
    reach = width // 2 + LANES
    diag = pl.pallas_call(
        diagonal_kernel,
        out_shape=jax.ShapeDtypeStruct((2, size, reach), I16),
        in_specs=[smem, smem] + [vmem] * (chips + len(row_parts)),
        out_specs=vmem,
        scratch_shapes=[pltpu.VMEM((size, width), F32)],
        compiler_params=pltpu.CompilerParams(vmem_limit_bytes=16 << 20),
        name="diagonal",
    )(place, where, *coded, *row_parts)

    sums = [coded[0]]
    for shifts in ((6, 5), (7, 2, 4, 1, 3)):
        for j in shifts:
            to = [
                (h * NY + y, (h + j // NY) % NH * NY + (y + j) % NY)
                for h in range(NH)
                for y in range(NY)
            ]
            sums.append(lax.ppermute(coded[j], HY, to))
    slab = jax.ShapeDtypeStruct((size // NC, width), BF16)
    mine, theirs = pl.pallas_call(
        finish_kernel,
        out_shape=[slab, slab],
        in_specs=[smem, smem] + [vmem] * len(sums),
        out_specs=[vmem] * 2,
        compiler_params=pltpu.CompilerParams(vmem_limit_bytes=12 << 20),
        name="finish",
    )(place, where, *sums)

    theirs = lax.ppermute(theirs, "c", CORE_SWAP)
    column_block = jnp.where(
        core == 0,
        jnp.concatenate([mine, theirs], axis=1),
        jnp.concatenate([theirs, mine], axis=1),
    )

    diag = diag.reshape(pieces, depth, reach)
    diag = lax.all_to_all(diag, CHIPS, split_axis=0, concat_axis=0, tiled=True)
    index = group * chips + chip
    inverse = lax.dynamic_slice(
        diag_inverse,
        (core * members, index % (pieces // 2) * depth, 0),
        (members, depth, size),
    )
    inverse = jnp.transpose(inverse, (1, 0, 2)).reshape(depth, 2, width // 2)
    inverse = lax.dynamic_index_in_dim(inverse, index // (pieces // 2), 1, keepdims=False)
    piece = pl.pallas_call(
        piece_kernel,
        out_shape=jax.ShapeDtypeStruct((pieces * NC, depth, reach), I16),
        in_specs=[vmem, vmem],
        out_specs=vmem,
        compiler_params=pltpu.CompilerParams(vmem_limit_bytes=6 << 20),
        name="piece",
    )(diag, inverse)
    whole = lax.all_to_all(piece, CHIPS + ("c",), split_axis=0, concat_axis=0, tiled=True)
    diagonal = pl.pallas_call(
        total_kernel,
        out_shape=jax.ShapeDtypeStruct(diag_inverse.shape, F32),
        in_specs=[vmem],
        out_specs=vmem,
        compiler_params=pltpu.CompilerParams(vmem_limit_bytes=12 << 20),
        name="total",
    )(whole.reshape(pieces, NC, depth, reach))
    return column_block, diagonal


def solution(mesh):
    fine = Mesh(mesh.devices.reshape(NX, NL, NH, NY, NC), ("x", "l", "h", "y", "c"))
    return jax.shard_map(
        update,
        mesh=fine,
        in_specs=(P(XL, ("h", "y", "c")), P(("h", "y", "c")), P(), P(), P()),
        out_specs=(P(("x", "l", "h", "y", "c")), P()),
        check_vma=False,
    )
```
